256 devices in a mesh: ax: 32 (over x, y, core), az: 8 (over z).
Axes of the slice: x: 4, y: 4, z: 8, core: 2. Of those that a mesh axis runs over, the one named last changes fastest.
Arguments:
- initial_state: float32 [16, 5, 64, 64, 128], P(None, None, 'ax', 'az'), may hold values from -6 to 6
- forcing: float32 [16, 5, 64, 64, 128], P(None, None, 'ax', 'az'), may hold values from -12 to 12
- axial_speed: float32 [64, 64, 128], P('ax', 'az'), may hold values from 0.2 to 1
- swirl_speed: float32 [64, 64, 128], P('ax', 'az'), may hold values from -0.5 to 0.5
- coupling: float32 [5, 5, 64, 64, 128], P(None, None, 'ax', 'az'), may hold values from -1.5 to 1.5
Outputs:
- final_state: float32 [16, 5, 64, 64, 128], P(None, None, 'ax', 'az')
- basis: float32 [8, 16, 2, 5, 64, 64, 128], P(None, None, None, None, 'ax', 'az')
- upper: float32 [8, 16, 16], replicated
The draws below stay inside these ranges and needn't reach their ends.
All inputs are finite; a program needn't handle non-finite values.
Results may differ from the reference program's by a relative error of at most 0.0001.
Values sent between devices are 32-bit elements; how exact they have to be, the bound alone decides.
No kernel may reach another device: no remote copies, remote signals or barrier semaphores. Data moves between devices by JAX's collectives and lax.ppermute only.
A program may use at most 64 MiB of HBM per device.

```python
import math
import jax
import jax.numpy as jnp
import numpy as np
from jax import lax

CR = 128
NFORCE = 16
NVAR = 5
NFREQ = 8
STEPS = 2
NX = 64
NT = 64


def draw_forcing(key, part):
    shape = (NFORCE, NVAR, NX, NT, CR)
    ramp = 3.0 ** (jnp.arange(NX, dtype=jnp.float32) / max(NX - 1, 1))
    ramp = ramp[None, None, :, None, None]
    base = jnp.clip(jax.random.normal(key, shape, jnp.float32), -4.0, 4.0)
    return (base * ramp).astype(jnp.float32)


def levels(key, extent, cuts, least, top_value):
    loudness = 1.0
    for dim, blocks in cuts:
        draws = jax.random.uniform(jax.random.fold_in(jax.random.fold_in(key, 6), dim), (blocks,), jnp.float32, least / len(cuts), top_value / len(cuts))
        loudness = loudness * jnp.repeat(jnp.exp(draws), extent[dim] // blocks).reshape((-1,) + (1,) * (len(extent) - 1 - dim))
    return loudness


def scatter_about(own_key, dims, spread, most, pieces=(), kind=jnp.bfloat16):
    factor_of = levels(own_key, dims, pieces, -0.22, 0.18) if pieces else 1.0
    entries = jax.random.normal(own_key, dims, jnp.float32) * spread * factor_of
    return jnp.minimum(jnp.maximum(entries, -most), most).astype(kind)


def setup_inputs(seed: int = 0) -> dict:
    splits = jax.random.split(jax.random.key(seed), 6)
    initial_state = scatter_about(splits[0], (NFORCE, NVAR, NX, NT, CR), 1.0, 6.0, ((2, 32), (3, 8)), jnp.float32)
    forcing = draw_forcing(jax.random.fold_in(splits[5], 71), 0)
    axial_speed = jnp.clip(0.2 + 0.8 * jax.random.uniform(splits[2], (NX, NT, CR), jnp.float32) ** levels(splits[2], (NX, NT, CR), ((0, 32), (1, 8)), -0.2, 0.2), 0.2, 1.0)
    swirl_speed = jnp.clip(jax.random.uniform(splits[3], (NX, NT, CR), jnp.float32, -0.5, 0.5) * levels(splits[3], (NX, NT, CR), ((0, 32), (1, 8)), -0.4, 0.0), -0.5, 0.5)
    coupling = scatter_about(splits[4], (NVAR, NVAR, NX, NT, CR), 0.3, 1.5, ((2, 32), (3, 8)), jnp.float32)
    return {"initial_state": initial_state, "forcing": forcing, "axial_speed": axial_speed, "swirl_speed": swirl_speed, "coupling": coupling}


step_size = 0.25
viscous = 0.1

def frequencies():
    return [0.4 * (k + 1) for k in range(NFREQ)]

def forcing_time(moment):
    return sum((math.cos(w * moment) for w in frequencies()))

def assemble(state, ext_x, ext_t, axial_speed, swirl_speed, coupling, forcing, gval):
    x_plus = ext_x[:, :, 2:]
    x_minus = ext_x[:, :, :-2]
    t_plus = ext_t[:, :, :, 2:]
    t_minus = ext_t[:, :, :, :-2]
    radial = jnp.pad(state, ((0, 0), (0, 0), (0, 0), (0, 0), (1, 1)))
    ddx = 0.5 * (x_plus - x_minus)
    ddt = 0.5 * (t_plus - t_minus)
    lap = x_plus + x_minus + t_plus + t_minus + radial[..., 2:] + radial[..., :-2] - 6.0 * state
    mixing = jnp.sum(coupling[None] * state[:, None], axis=2)
    result = -axial_speed * ddx - swirl_speed * ddt + viscous * lap + mixing + gval * forcing
    result = result.at[:, 1].add(-ddx[:, 4])
    result = result.at[:, 2].add(-ddt[:, 4])
    result = result.at[:, 4].add(-(ddx[:, 1] + ddt[:, 2]))
    return result

def tendency(state, axial_speed, swirl_speed, coupling, forcing, gval):
    ext_x = jnp.pad(state, ((0, 0), (0, 0), (1, 1), (0, 0), (0, 0)))
    ext_t = jnp.concatenate([state[:, :, :, -1:], state, state[:, :, :, :1]], axis=3)
    return assemble(state, ext_x, ext_t, axial_speed, swirl_speed, coupling, forcing, gval)

def fourier_weights(moment):
    table = np.array([[math.cos(w * moment) * step_size, -math.sin(w * moment) * step_size] for w in frequencies()])
    return jnp.asarray(table, dtype=jnp.float32)

def reference(initial_state, forcing, axial_speed, swirl_speed, coupling):
    state = initial_state
    shape = (NFREQ, NFORCE, 2, NVAR) + initial_state.shape[2:]
    accum = jnp.zeros(shape, jnp.float32)
    for step in range(STEPS):
        moment = step * step_size
        half = moment + 0.5 * step_size
        whole = moment + step_size
        args = (axial_speed, swirl_speed, coupling, forcing)
        k_one = tendency(state, *args, forcing_time(moment))
        k_two = tendency(state + 0.5 * step_size * k_one, *args, forcing_time(half))
        k_three = tendency(state + 0.5 * step_size * k_two, *args, forcing_time(half))
        k_four = tendency(state + step_size * k_three, *args, forcing_time(whole))
        state = state + step_size / 6.0 * (k_one + 2.0 * k_two + 2.0 * k_three + k_four)
        weights = fourier_weights(whole)
        accum = accum + weights[:, None, :, None, None, None, None] * state[None, :, None]
    cells = float(initial_state.shape[2] * initial_state.shape[3] * initial_state.shape[4])

    def per_freq(block):
        matrix = block.reshape(NFORCE, -1)
        gram = jnp.dot(matrix, matrix.T, precision=lax.Precision.HIGHEST) / cells
        lower = jnp.linalg.cholesky(gram)
        solved = jax.scipy.linalg.solve_triangular(lower, matrix, lower=True)
        return (solved.reshape(block.shape), lower.T)
    basis, upper = lax.map(per_freq, accum)
    return (state, basis, upper)
```

```python
import math

import jax
import jax.numpy as jnp
import numpy as np
from jax import lax
from jax.experimental import pallas as pl
from jax.experimental.pallas import tpu as pltpu
from jax.sharding import PartitionSpec as P

NFORCE = 16
NVAR = 5
NFREQ = 8
STEPS = 2
ROWS = NFORCE * NVAR * 8
step_size = 0.25
viscous = 0.1
F32, BF16 = jnp.float32, jnp.bfloat16
VMEM = pl.BlockSpec(memory_space=pltpu.VMEM)
LIMIT = 48 << 20


def frequencies():
    return [0.4 * (k + 1) for k in range(NFREQ)]


def forcing_time(moment):
    return sum(math.cos(w * moment) for w in frequencies())


def call(body, outs, cost, **kw):
    shapes = [jax.ShapeDtypeStruct(s, d) for s, d in outs]
    return pl.pallas_call(
        body,
        out_shape=shapes,
        compiler_params=pltpu.CompilerParams(vmem_limit_bytes=LIMIT),
        cost_estimate=pl.CostEstimate(flops=cost, bytes_accessed=cost, transcendentals=0),
        **kw,
    )


def parities():
    return lax.rem(lax.axis_index("ax"), 2), lax.rem(lax.axis_index("az"), 2)


def pack_rows(outer, inner, odd, first, second):
    for half, ref in enumerate((outer, inner)):
        low = ref[pl.ds(0, 80, stride=8), :]
        high = ref[pl.ds(7, 80, stride=8), :]
        where = pl.ds(half * 80, 80)
        first[where, :] = jnp.where(odd == 0, high, low)
        second[where, :] = jnp.where(odd == 0, low, high)


def split_state(state, outer, inner, first, second):
    odd_x, odd_z = parities()

    def one(j, carry):
        for v in range(NVAR):
            rows = pl.ds(pl.multiple_of(j * 40 + v * 8, 8), 8)
            outer[rows, :] = state[j, v, odd_x]
            inner[rows, :] = state[j, v, 1 - odd_x]
        return carry

    lax.fori_loop(0, NFORCE, one, 0, unroll=4)
    pack_rows(outer, inner, odd_z, first, second)


def split_fixed(forcing, axial, swirl, coupling, f_out, f_in, c_out, c_in, s_out, s_in):
    odd_x, _ = parities()
    sign = jnp.where(odd_x == 0, 1.0, -1.0)

    def one(j, carry):
        for v in range(NVAR):
            rows = pl.ds(pl.multiple_of(j * 40 + v * 8, 8), 8)
            f_out[rows, :] = forcing[j, v, odd_x]
            f_in[rows, :] = forcing[j, v, 1 - odd_x]
        return carry

    lax.fori_loop(0, NFORCE, one, 0, unroll=4)
    for layer, c, s, toward in ((odd_x, c_out, s_out, -sign), (1 - odd_x, c_in, s_in, sign)):
        for v in range(NVAR):
            for w in range(NVAR):
                shift = 6.0 * viscous if v == w else 0.0
                c[pl.ds((v * NVAR + w) * 8, 8), :] = coupling[v, w, layer] - shift
        s[0:8, :] = axial[layer] * (0.5 * toward)
        s[8:16, :] = swirl[layer] * 0.5


def layer_body(inner, stage, gval, refs):
    (own, other, recv, z1, z2, forcing, coupling, speed), rest = refs[:8], refs[8:]
    odd_x, odd_z = parities()
    sign = jnp.where(odd_x == 0, 0.5, -0.5)
    if not inner:
        sign = -sign
    sub = lax.broadcasted_iota(jnp.int32, (8, 128), 0)
    lane = lax.broadcasted_iota(jnp.int32, (8, 128), 1)
    row0, row7, lane0, lane127 = sub == 0, sub == 7, lane == 0, lane == 127
    pick = (sub < 4) == (odd_z == 1)
    base = 80 if inner else 0
    adv, swr = speed[0:8, :], speed[8:16, :]
    if stage == 1:
        start, (out,) = own, rest[:1]
    elif stage in (2, 3):
        start, (out,) = rest[0], rest[1:2]
    else:
        start, y2, y3, out = rest[:4]

    def one(j, carry):
        at = pl.multiple_of(j * 40, 8)
        rows = [pl.ds(at + v * 8, 8) for v in range(NVAR)]
        y = [own[r, :] for r in rows]
        dx, dt, rate = [], [], []
        for v in range(NVAR):
            a, b = other[rows[v], :], recv[rows[v], :]
            n = base + j * NVAR + v
            edge = jnp.where(
                pick,
                jnp.broadcast_to(z1[pl.ds(n, 1), :], (8, 128)),
                jnp.broadcast_to(z2[pl.ds(n, 1), :], (8, 128)),
            )
            tm = jnp.where(row0, edge, pltpu.roll(y[v], 1, 0))
            tp = jnp.where(row7, edge, pltpu.roll(y[v], 7, 0))
            rm = jnp.where(lane0, 0.0, pltpu.roll(y[v], 1, 1))
            rp = jnp.where(lane127, 0.0, pltpu.roll(y[v], 127, 1))
            dx.append(b - a)
            dt.append(tp - tm)
            lap = (a + b) + (tm + tp) + (rm + rp)
            total = viscous * lap + gval * forcing[rows[v], :] - adv * dx[v] - swr * dt[v]
            for w in range(NVAR):
                total = total + coupling[(v * NVAR + w) * 8 : (v * NVAR + w) * 8 + 8, :] * y[w]
            rate.append(total)
        rate[1] = rate[1] - sign * dx[4]
        rate[2] = rate[2] - 0.5 * dt[4]
        rate[4] = rate[4] - (sign * dx[1] + 0.5 * dt[2])
        for v in range(NVAR):
            q = y[v] if stage == 1 else start[rows[v], :]
            if stage < 4:
                weight = step_size if stage == 3 else 0.5 * step_size
                out[rows[v], :] = q + weight * rate[v]
            else:
                mean = (y2[rows[v], :] - q) + (2.0 * y3[rows[v], :] + y[v])
                out[rows[v], :] = mean * (1.0 / 3.0) + (step_size / 6.0) * rate[v]
        return carry

    lax.fori_loop(0, NFORCE, one, 0, unroll=2)


def outer_layer(stage, gval, *args):
    def body(*refs):
        layer_body(False, stage, gval, refs)

    return call(body, [((ROWS, 128), F32)], 1 << 20, in_specs=[VMEM] * len(args), out_specs=[VMEM])(*args)[0]


def inner_layer(stage, gval, new_outer, *args):
    def body(done, *refs):
        layer_body(True, stage, gval, refs)
        _, odd_z = parities()
        pack_rows(done, refs[-3], odd_z, refs[-2], refs[-1])

    return call(
        body,
        [((ROWS, 128), F32), ((160, 128), F32), ((160, 128), F32)],
        1 << 20,
        in_specs=[VMEM] * (len(args) + 1),
        out_specs=[VMEM] * 3,
    )(new_outer, *args)


def swaps():
    core = [(i, i ^ 1) for i in range(32)]
    chip = [(i, i + 1) for i in range(1, 31, 2)]
    chip += [(b, a) for a, b in chip]
    z1 = [(i, i ^ 1) for i in range(8)]
    z2 = [(i, (i + 1) % 8) for i in range(1, 8, 2)]
    z2 += [(b, a) for a, b in z2]
    return core, chip, z1, z2


def three_parts(x):
    high = x.astype(BF16)
    rest = x - high.astype(F32)
    mid = rest.astype(BF16)
    low = (rest - mid.astype(F32)).astype(BF16)
    return high, mid, low


def gram_body(first_out, first_in, last_out, last_in, final, parts, packed, sem):
    odd_x, _ = parities()
    copies = [
        pltpu.make_async_copy(ref, final.at[:, :, at], sem.at[i])
        for i, (ref, at) in enumerate(((last_out, odd_x), (last_in, 1 - odd_x)))
    ]
    for copy in copies:
        copy.start()
    layers = ((first_out, last_out), (first_in, last_in))
    total = jnp.zeros((96, 96), F32)
    for v in range(NVAR):
        for half, pair in enumerate(layers):
            for t in range(8):
                lanes = pl.ds(half * 1024 + t * 128, 128)
                for n, ref in enumerate(pair):
                    x = ref.reshape(ROWS, 128)[pl.ds(v * 8 + t, NFORCE, stride=40), :]
                    high, mid, low = three_parts(x)
                    for place, part in enumerate((high, mid, low, high, mid, high)):
                        parts[v, pl.ds(place * 32 + n * 16, 16), lanes] = part
        block = parts[v, 0:96, :]
        total = total + lax.dot_general(
            block, block, (((1,), (1,)), ((), ())), preferred_element_type=F32
        )
    small = total[0:32] + total[32:64] + total[64:96]
    small = small[:, 0:32] + small[:, 32:64] + small[:, 64:96]
    flat = jnp.concatenate([small[8 * a : 8 * a + 8] for a in range(4)], axis=1)
    for i in range(32):
        packed[i] = flat
    for copy in copies:
        copy.wait()


def gram_parts(first_out, first_in, last_out, last_in):
    cube = lambda x: x.reshape(NFORCE, NVAR, 8, 128)
    return call(
        gram_body,
        [
            ((NFORCE, NVAR, 2, 8, 128), F32),
            ((NVAR, 192, 2048), BF16),
            ((32, 8, 128), F32),
        ],
        1 << 22,
        in_specs=[VMEM] * 4,
        out_specs=[pl.BlockSpec(memory_space=pl.ANY), VMEM, VMEM],
        scratch_shapes=[pltpu.SemaphoreType.DMA((2,))],
    )(*map(cube, (first_out, first_in, last_out, last_in)))


def lane_tables():
    rows = []
    for k, w in enumerate(frequencies()):
        for j in range(NFORCE):
            for c in range(2):
                f = math.cos if c == 0 else (lambda a: -math.sin(a))
                rows.append(
                    (
                        math.cos(w * step_size),
                        float(j),
                        f(w * step_size) * step_size,
                        f(w * 2 * step_size) * step_size,
                    )
                )
    table = np.zeros((8, 256), np.float32)
    table[:4] = np.array(rows).T
    return table


def factor(gathered, table, weights, upper, work):
    gram = gathered[0]
    for i in range(1, 8):
        gram = gram + gathered[i]
    cells = 64.0 * 64.0 * 128.0
    gram = gram * (step_size * step_size / cells)
    both = gram + pltpu.roll(gram, 48, 1)
    cross = pltpu.roll(gram, 112, 1) + pltpu.roll(gram, 64, 1)
    cosine = table[0:1, :]
    wanted = table[1:2, :]
    rows, inv = [], []
    sub = lax.broadcasted_iota(jnp.int32, (16, 256), 0)
    for i in range(NFORCE):
        column = lambda m: jnp.concatenate(
            [jnp.broadcast_to(m[:, a * 32 + i : a * 32 + i + 1], (8, 256)) for a in range(2)], axis=0
        )
        rows.append(column(both) + cosine * column(cross))
        inv.append(jnp.where(sub == i, 1.0, 0.0))
    low = jnp.zeros((16, 256), F32)
    up = jnp.zeros((16, 256), F32)
    for p in range(NFORCE):
        pivot = rows[p][p : p + 1, :]
        scaled = rows[p] * (1.0 / pivot)
        root = lax.rsqrt(pivot)
        root = root * (1.5 - 0.5 * pivot * root * root)
        mine = wanted == float(p)
        low = jnp.where(mine, inv[p] * root, low)
        up = jnp.where(mine & (sub >= p), rows[p] * root, up)
        for i in range(p + 1, NFORCE):
            m = scaled[i : i + 1, :]
            rows[i] = rows[i] - m * rows[p]
            inv[i] = inv[i] - m * inv[p]
    side = jnp.concatenate([low * table[2:3, :], low * table[3:4, :]], axis=0)
    high, mid, tail = (x.astype(F32) for x in three_parts(side))
    stack = jnp.concatenate([high, high, high, mid, mid, tail, up, jnp.zeros((48, 256), F32)], axis=0)
    turned = stack.T
    weights[...] = turned[:, 0:192].astype(BF16)
    work[...] = turned[:, 128:256]
    upper[...] = work[pl.ds(0, 128, stride=2), :][:, 64:80].reshape(NFREQ, NFORCE, NFORCE)


def basis_body(gathered, table, parts, basis, upper, weights, work):
    @pl.when(pl.program_id(0) == 0)
    def _():
        factor(gathered, table, weights, upper, work)

    odd_x, _ = parities()
    flat = basis.reshape(256 * 16, 128)
    for half in range(2):
        at = odd_x if half == 0 else 1 - odd_x
        for t in range(0, 8, 2):
            lanes = pl.ds(half * 1024 + t * 128, 256)
            block = jnp.dot(weights[...], parts[0, :, lanes], preferred_element_type=F32)
            for u in range(2):
                flat[pl.ds(at * 8 + t + u, 256, stride=16), :] = block[:, u * 128 : u * 128 + 128]


def basis_of(gathered, parts):
    whole = lambda *shape: pl.BlockSpec(shape, lambda v: (0,) * len(shape))
    return pl.pallas_call(
        basis_body,
        grid=(NVAR,),
        out_shape=[
            jax.ShapeDtypeStruct((NFREQ, NFORCE, 2, NVAR, 2, 8, 128), F32),
            jax.ShapeDtypeStruct((NFREQ, NFORCE, NFORCE), F32),
        ],
        in_specs=[
            whole(8, 8, 128),
            whole(8, 256),
            pl.BlockSpec((1, 192, 2048), lambda v: (v, 0, 0)),
        ],
        out_specs=[
            pl.BlockSpec((NFREQ, NFORCE, 2, 1, 2, 8, 128), lambda v: (0, 0, 0, v, 0, 0, 0)),
            whole(NFREQ, NFORCE, NFORCE),
        ],
        scratch_shapes=[pltpu.VMEM((256, 192), BF16), pltpu.VMEM((256, 128), F32)],
        compiler_params=pltpu.CompilerParams(vmem_limit_bytes=LIMIT),
    )(gathered, jnp.asarray(lane_tables()), parts)


def on_device(initial_state, forcing, axial_speed, swirl_speed, coupling):
    core, chip, z1, z2 = swaps()
    layer, rows = ((ROWS, 128), F32), ((160, 128), F32)
    outer, inner, first, second = call(
        split_state, [layer, layer, rows, rows], 1 << 20, in_specs=[VMEM], out_specs=[VMEM] * 4
    )(initial_state)
    c, s = ((200, 128), F32), ((16, 128), F32)
    f_out, f_in, c_out, c_in, s_out, s_in = call(
        split_fixed, [layer, layer, c, c, s, s], 1 << 20, in_specs=[VMEM] * 4, out_specs=[VMEM] * 6
    )(forcing, axial_speed, swirl_speed, coupling)

    kept = []
    for step in range(STEPS):
        moment = step * step_size
        times = (moment, moment + 0.5 * step_size, moment + 0.5 * step_size, moment + step_size)
        base = (outer, inner)
        history = []
        for stage in range(1, 5):
            gval = forcing_time(times[stage - 1])
            from_chip = lax.ppermute(outer, "ax", chip)
            from_core = lax.ppermute(inner, "ax", core)
            r1 = lax.ppermute(first, "az", z1)
            r2 = lax.ppermute(second, "az", z2)
            if stage == 1:
                more = ((), ())
            elif stage < 4:
                more = ((base[0],), (base[1],))
            else:
                more = tuple((base[i], history[0][i], history[1][i]) for i in range(2))
            new_outer = outer_layer(stage, gval, outer, inner, from_chip, r1, r2, f_out, c_out, s_out, *more[0])
            new_inner, first, second = inner_layer(
                stage, gval, new_outer, inner, outer, from_core, r1, r2, f_in, c_in, s_in, *more[1]
            )
            outer, inner = new_outer, new_inner
            history.append((outer, inner))
        kept.append((outer, inner))
    final, parts, packed = gram_parts(*kept[0], *kept[1])
    gathered = lax.all_to_all(packed, "ax", 0, 0, tiled=True)
    partial = jnp.broadcast_to(jnp.sum(gathered, axis=0)[None], (8, 8, 128))
    gathered = lax.all_to_all(partial, "az", 0, 0, tiled=True)
    basis, upper = basis_of(gathered, parts)
    return final, basis, upper


def solution(mesh):
    return jax.shard_map(
        on_device,
        mesh=mesh,
        in_specs=(
            P(None, None, "ax", "az", None),
            P(None, None, "ax", "az", None),
            P("ax", "az", None),
            P("ax", "az", None),
            P(None, None, "ax", "az", None),
        ),
        out_specs=(
            P(None, None, "ax", "az", None),
            P(None, None, None, None, "ax", "az", None),
            P(),
        ),
        check_vma=False,
    )
```

```python
import math

import jax
import jax.numpy as jnp
import numpy as np
from jax import lax
from jax.experimental import pallas as pl
from jax.experimental.pallas import tpu as pltpu
from jax.sharding import PartitionSpec as P

NFORCE = 16
NVAR = 5
NFREQ = 8
STEPS = 2
ROWS = NFORCE * NVAR * 8
step_size = 0.25
viscous = 0.1
F32, BF16 = jnp.float32, jnp.bfloat16
VMEM = pl.BlockSpec(memory_space=pltpu.VMEM)
LIMIT = 48 << 20
UNROLL = 4


def frequencies():
    return [0.4 * (k + 1) for k in range(NFREQ)]


def forcing_time(moment):
    return sum(math.cos(w * moment) for w in frequencies())


def call(body, outs, cost, **kw):
    shapes = [jax.ShapeDtypeStruct(s, d) for s, d in outs]
    return pl.pallas_call(
        body,
        out_shape=shapes,
        compiler_params=pltpu.CompilerParams(vmem_limit_bytes=LIMIT),
        cost_estimate=pl.CostEstimate(flops=cost, bytes_accessed=cost, transcendentals=0),
        **kw,
    )


def parities():
    return lax.rem(lax.axis_index("ax"), 2), lax.rem(lax.axis_index("az"), 2)


def pack_rows(outer, inner, odd, first, second):
    for half, ref in enumerate((outer, inner)):
        low = ref[pl.ds(0, 80, stride=8), :]
        high = ref[pl.ds(7, 80, stride=8), :]
        where = pl.ds(half * 80, 80)
        first[where, :] = jnp.where(odd == 0, high, low)
        second[where, :] = jnp.where(odd == 0, low, high)


def split_state(state, outer, inner, first, second):
    odd_x, odd_z = parities()

    def one(j, carry):
        for v in range(NVAR):
            rows = pl.ds(pl.multiple_of(j * 40 + v * 8, 8), 8)
            outer[rows, :] = state[j, v, odd_x]
            inner[rows, :] = state[j, v, 1 - odd_x]
        return carry

    lax.fori_loop(0, NFORCE, one, 0, unroll=4)
    pack_rows(outer, inner, odd_z, first, second)


def split_fixed(forcing, axial, swirl, coupling, f_out, f_in, c_out, c_in, s_out, s_in):
    odd_x, _ = parities()
    sign = jnp.where(odd_x == 0, 1.0, -1.0)

    def one(j, carry):
        for v in range(NVAR):
            rows = pl.ds(pl.multiple_of(j * 40 + v * 8, 8), 8)
            f_out[rows, :] = forcing[j, v, odd_x]
            f_in[rows, :] = forcing[j, v, 1 - odd_x]
        return carry

    lax.fori_loop(0, NFORCE, one, 0, unroll=4)
    for layer, c, s, toward in ((odd_x, c_out, s_out, -sign), (1 - odd_x, c_in, s_in, sign)):
        for v in range(NVAR):
            for w in range(NVAR):
                shift = 6.0 * viscous if v == w else 0.0
                c[pl.ds((v * NVAR + w) * 8, 8), :] = coupling[v, w, layer] - shift
        s[0:8, :] = axial[layer] * (0.5 * toward)
        s[8:16, :] = swirl[layer] * 0.5


def layer_body(inner, stage, gval, refs):
    (own, other, recv, z1, z2, forcing, coupling, speed), rest = refs[:8], refs[8:]
    odd_x, odd_z = parities()
    sign = jnp.where(odd_x == 0, 0.5, -0.5)
    if not inner:
        sign = -sign
    sub = lax.broadcasted_iota(jnp.int32, (8, 128), 0)
    lane = lax.broadcasted_iota(jnp.int32, (8, 128), 1)
    row0, row7 = sub == 0, sub == 7
    from_low = jnp.where(lane == 0, 0.0, viscous)
    from_high = jnp.where(lane == 127, 0.0, viscous)
    pick = (sub < 4) == (odd_z == 1)
    base = 80 if inner else 0
    adv, swr = speed[0:8, :], speed[8:16, :]
    c_other, c_recv = viscous + adv, viscous - adv
    c_minus, c_plus = viscous + swr, viscous - swr
    edge_of_domain = None
    if not inner:
        position = lax.axis_index("ax")
        inside = jnp.where((position > 0) & (position < 31), 1.0, 0.0)
        c_recv = c_recv * inside
        edge_of_domain = sign * inside
    c_dx = sign if inner else edge_of_domain
    if stage == 1:
        start, (out,) = own, rest[:1]
    elif stage in (2, 3):
        start, (out,) = rest[0], rest[1:2]
    else:
        start, y2, y3, out = rest[:4]
    group = 2

    def one(block, carry):
        at = [pl.multiple_of((block * group + g) * 40, 8) for g in range(group)]
        y = [[own[pl.ds(at[g] + v * 8, 8), :] for v in range(NVAR)] for g in range(group)]
        press = [{} for _ in range(group)]
        rate = [{} for _ in range(group)]
        for v in (4, 1, 2, 0, 3):
            for g in range(group):
                rows = pl.ds(at[g] + v * 8, 8)
                a, b = other[rows, :], recv[rows, :]
                n = base + (block * group + g) * NVAR + v
                edge = jnp.where(
                    pick,
                    jnp.broadcast_to(z1[pl.ds(n, 1), :], (8, 128)),
                    jnp.broadcast_to(z2[pl.ds(n, 1), :], (8, 128)),
                )
                me = y[g][v]
                tm = jnp.where(row0, edge, pltpu.roll(me, 1, 0))
                tp = jnp.where(row7, edge, pltpu.roll(me, 7, 0))
                if v in (1, 4):
                    press[g]["x", v] = b * c_dx - a * sign
                if v in (2, 4):
                    press[g]["t", v] = 0.5 * (tp - tm)
                rate[g][v] = (
                    (c_other * a + c_recv * b)
                    + (c_minus * tm + c_plus * tp)
                    + (from_low * pltpu.roll(me, 1, 1) + from_high * pltpu.roll(me, 127, 1))
                    + gval * forcing[rows, :]
                )
            for w in range(NVAR):
                c = coupling[(v * NVAR + w) * 8 : (v * NVAR + w) * 8 + 8, :]
                for g in range(group):
                    rate[g][v] = rate[g][v] + c * y[g][w]
        for g in range(group):
            rate[g][1] = rate[g][1] - press[g]["x", 4]
            rate[g][2] = rate[g][2] - press[g]["t", 4]
            rate[g][4] = rate[g][4] - (press[g]["x", 1] + press[g]["t", 2])
            for v in range(NVAR):
                rows = pl.ds(at[g] + v * 8, 8)
                q = y[g][v] if stage == 1 else start[rows, :]
                if stage < 4:
                    weight = step_size if stage == 3 else 0.5 * step_size
                    out[rows, :] = q + weight * rate[g][v]
                else:
                    mean = (y2[rows, :] - q) + (2.0 * y3[rows, :] + y[g][v])
                    out[rows, :] = mean * (1.0 / 3.0) + (step_size / 6.0) * rate[g][v]
        return carry

    lax.fori_loop(0, NFORCE // group, one, 0, unroll=UNROLL)


def outer_layer(stage, gval, *args):
    def body(*refs):
        layer_body(False, stage, gval, refs)

    return call(body, [((ROWS, 128), F32)], 1 << 20, in_specs=[VMEM] * len(args), out_specs=[VMEM])(*args)[0]


def inner_layer(stage, gval, new_outer, *args):
    def body(done, *refs):
        layer_body(True, stage, gval, refs)
        _, odd_z = parities()
        pack_rows(done, refs[-3], odd_z, refs[-2], refs[-1])

    return call(
        body,
        [((ROWS, 128), F32), ((160, 128), F32), ((160, 128), F32)],
        1 << 20,
        in_specs=[VMEM] * (len(args) + 1),
        out_specs=[VMEM] * 3,
    )(new_outer, *args)


def swaps():
    core = [(i, i ^ 1) for i in range(32)]
    chip = [(i, (i + 1) % 32) for i in range(1, 32, 2)]
    chip += [(b, a) for a, b in chip]
    z1 = [(i, i ^ 1) for i in range(8)]
    z2 = [(i, (i + 1) % 8) for i in range(1, 8, 2)]
    z2 += [(b, a) for a, b in z2]
    return core, chip, z1, z2


def three_parts(x):
    high = x.astype(BF16)
    rest = x - high.astype(F32)
    mid = rest.astype(BF16)
    low = (rest - mid.astype(F32)).astype(BF16)
    return high, mid, low


def split_rows(ref, first, stride, parts, n, lanes, places):
    split = three_parts(ref[pl.ds(first, NFORCE, stride=stride), :])
    for place in places:
        parts[pl.ds(place * 32 + n * 16, 16), lanes] = split[(0, 1, 2, 0, 1, 0)[place]]


def gram_body(first_out, first_in, last_out, last_in, middle, final, packed, parts, sem):
    odd_x, _ = parities()
    cube = lambda ref: ref.reshape(NFORCE, NVAR, 8, 128)
    copies = [
        pltpu.make_async_copy(cube(ref), to.at[:, :, at], sem.at[i])
        for i, (ref, to, at) in enumerate(
            (
                (first_out, middle, odd_x),
                (first_in, middle, 1 - odd_x),
                (last_out, final, odd_x),
                (last_in, final, 1 - odd_x),
            )
        )
    ]
    for copy in copies:
        copy.start()
    layers = ((first_out, last_out), (first_in, last_in))
    total = jnp.zeros((96, 96), F32)
    for v in range(NVAR):
        for half, pair in enumerate(layers):
            for t in range(8):
                lanes = pl.ds(half * 1024 + t * 128, 128)
                for n, ref in enumerate(pair):
                    split_rows(ref, v * 8 + t, 40, parts.at[v], n, lanes, (0, 1, 2))
        block = parts[v]
        total = total + lax.dot_general(
            block, block, (((1,), (1,)), ((), ())), preferred_element_type=F32
        )
    small = total[0:32] + total[32:64] + total[64:96]
    small = small[:, 0:32] + small[:, 32:64] + small[:, 64:96]
    flat = jnp.concatenate([small[8 * a : 8 * a + 8] for a in range(4)], axis=1)
    for i in range(32):
        packed[i] = flat
    for copy in copies:
        copy.wait()


def gram_parts(first_out, first_in, last_out, last_in):
    state = ((NFORCE, NVAR, 2, 8, 128), F32)
    return call(
        gram_body,
        [state, state, ((32, 8, 128), F32)],
        1 << 22,
        in_specs=[VMEM] * 4,
        out_specs=[pl.BlockSpec(memory_space=pl.ANY)] * 2 + [VMEM],
        scratch_shapes=[pltpu.VMEM((NVAR, 96, 2048), BF16), pltpu.SemaphoreType.DMA((4,))],
    )(first_out, first_in, last_out, last_in)


def lane_tables():
    rows = []
    for k, w in enumerate(frequencies()):
        for j in range(NFORCE):
            for c in range(2):
                f = math.cos if c == 0 else (lambda a: -math.sin(a))
                rows.append(
                    (
                        math.cos(w * step_size),
                        float(j),
                        f(w * step_size) * step_size,
                        f(w * 2 * step_size) * step_size,
                    )
                )
    table = np.zeros((8, 256), np.float32)
    table[:4] = np.array(rows).T
    return table


def factor(gathered, table, weights, upper, work):
    gram = gathered[0]
    for i in range(1, 8):
        gram = gram + gathered[i]
    cells = 64.0 * 64.0 * 128.0
    gram = gram * (step_size * step_size / cells)
    both = gram + pltpu.roll(gram, 48, 1)
    cross = pltpu.roll(gram, 112, 1) + pltpu.roll(gram, 64, 1)
    cosine = table[0:1, :]
    wanted = table[1:2, :]
    rows, inv = [], []
    sub = lax.broadcasted_iota(jnp.int32, (16, 256), 0)
    for i in range(NFORCE):
        column = lambda m: jnp.concatenate(
            [jnp.broadcast_to(m[:, a * 32 + i : a * 32 + i + 1], (8, 256)) for a in range(2)], axis=0
        )
        rows.append(column(both) + cosine * column(cross))
        inv.append(jnp.where(sub == i, 1.0, 0.0))
    low = jnp.zeros((16, 256), F32)
    up = jnp.zeros((16, 256), F32)
    for p in range(NFORCE):
        pivot = rows[p][p : p + 1, :]
        scaled = rows[p] * (1.0 / pivot)
        root = lax.rsqrt(pivot)
        root = root * (1.5 - 0.5 * pivot * root * root)
        mine = wanted == float(p)
        low = jnp.where(mine, inv[p] * root, low)
        up = jnp.where(mine & (sub >= p), rows[p] * root, up)
        for i in range(p + 1, NFORCE):
            m = scaled[i : i + 1, :]
            rows[i] = rows[i] - m * rows[p]
            inv[i] = inv[i] - m * inv[p]
    side = jnp.concatenate([low * table[2:3, :], low * table[3:4, :]], axis=0)
    high, mid, tail = (x.astype(F32) for x in three_parts(side))
    stack = jnp.concatenate([high, high, high, mid, mid, tail, up, jnp.zeros((48, 256), F32)], axis=0)
    turned = stack.T
    weights[...] = turned[:, 0:192].astype(BF16)
    work[...] = turned[:, 128:256]
    upper[...] = work[pl.ds(0, 128, stride=2), :][:, 64:80].reshape(NFREQ, NFORCE, NFORCE)


def basis_body(gathered, table, middle, final, basis, upper, weights, work, parts):
    for n, ref in enumerate((middle, final)):
        for x in range(2):
            for t in range(8):
                lanes = pl.ds(x * 1024 + t * 128, 128)
                split_rows(ref.reshape(256, 128), x * 8 + t, 16, parts, n, lanes, range(6))

    @pl.when(pl.program_id(0) == 0)
    def _():
        factor(gathered, table, weights, upper, work)

    flat = basis.reshape(256 * 16, 128)
    for x in range(2):
        for t in range(0, 8, 2):
            lanes = pl.ds(x * 1024 + t * 128, 256)
            block = jnp.dot(weights[...], parts[:, lanes], preferred_element_type=F32)
            for u in range(2):
                flat[pl.ds(x * 8 + t + u, 256, stride=16), :] = block[:, u * 128 : u * 128 + 128]


def basis_of(gathered, middle, final):
    whole = lambda *shape: pl.BlockSpec(shape, lambda v: (0,) * len(shape))
    field = pl.BlockSpec((NFORCE, 1, 2, 8, 128), lambda v: (0, v, 0, 0, 0))
    return pl.pallas_call(
        basis_body,
        grid=(NVAR,),
        out_shape=[
            jax.ShapeDtypeStruct((NFREQ, NFORCE, 2, NVAR, 2, 8, 128), F32),
            jax.ShapeDtypeStruct((NFREQ, NFORCE, NFORCE), F32),
        ],
        in_specs=[whole(8, 8, 128), whole(8, 256), field, field],
        out_specs=[
            pl.BlockSpec((NFREQ, NFORCE, 2, 1, 2, 8, 128), lambda v: (0, 0, 0, v, 0, 0, 0)),
            whole(NFREQ, NFORCE, NFORCE),
        ],
        scratch_shapes=[
            pltpu.VMEM((256, 192), BF16),
            pltpu.VMEM((256, 128), F32),
            pltpu.VMEM((192, 2048), BF16),
        ],
        compiler_params=pltpu.CompilerParams(vmem_limit_bytes=LIMIT),
    )(gathered, jnp.asarray(lane_tables()), middle, final)


def on_device(initial_state, forcing, axial_speed, swirl_speed, coupling):
    core, chip, z1, z2 = swaps()
    layer, rows = ((ROWS, 128), F32), ((160, 128), F32)
    outer, inner, first, second = call(
        split_state, [layer, layer, rows, rows], 1 << 20, in_specs=[VMEM], out_specs=[VMEM] * 4
    )(initial_state)
    c, s = ((200, 128), F32), ((16, 128), F32)
    f_out, f_in, c_out, c_in, s_out, s_in = call(
        split_fixed, [layer, layer, c, c, s, s], 1 << 20, in_specs=[VMEM] * 4, out_specs=[VMEM] * 6
    )(forcing, axial_speed, swirl_speed, coupling)

    kept = []
    for step in range(STEPS):
        moment = step * step_size
        times = (moment, moment + 0.5 * step_size, moment + 0.5 * step_size, moment + step_size)
        base = (outer, inner)
        history = []
        for stage in range(1, 5):
            gval = forcing_time(times[stage - 1])
            from_chip = lax.ppermute(outer, "ax", chip)
            from_core = lax.ppermute(inner, "ax", core)
            r1 = lax.ppermute(first, "az", z1)
            r2 = lax.ppermute(second, "az", z2)
            if stage == 1:
                more = ((), ())
            elif stage < 4:
                more = ((base[0],), (base[1],))
            else:
                more = tuple((base[i], history[0][i], history[1][i]) for i in range(2))
            new_outer = outer_layer(stage, gval, outer, inner, from_chip, r1, r2, f_out, c_out, s_out, *more[0])
            new_inner, first, second = inner_layer(
                stage, gval, new_outer, inner, outer, from_core, r1, r2, f_in, c_in, s_in, *more[1]
            )
            outer, inner = new_outer, new_inner
            history.append((outer, inner))
        kept.append((outer, inner))
    middle, final, packed = gram_parts(*kept[0], *kept[1])
    gathered = lax.all_to_all(packed, "ax", 0, 0, tiled=True)
    partial = jnp.broadcast_to(jnp.sum(gathered, axis=0)[None], (8, 8, 128))
    gathered = lax.all_to_all(partial, "az", 0, 0, tiled=True)
    basis, upper = basis_of(gathered, middle, final)
    return final, basis, upper


def solution(mesh):
    return jax.shard_map(
        on_device,
        mesh=mesh,
        in_specs=(
            P(None, None, "ax", "az", None),
            P(None, None, "ax", "az", None),
            P("ax", "az", None),
            P("ax", "az", None),
            P(None, None, "ax", "az", None),
        ),
        out_specs=(
            P(None, None, "ax", "az", None),
            P(None, None, None, None, "ax", "az", None),
            P(),
        ),
        check_vma=False,
    )
```

```python
import math

import jax
import jax.numpy as jnp
import numpy as np
from jax import lax
from jax.experimental import pallas as pl
from jax.experimental.pallas import tpu as pltpu
from jax.sharding import PartitionSpec as P

NFORCE = 16
NVAR = 5
NFREQ = 8
STEPS = 2
ROWS = NFORCE * NVAR * 8
step_size = 0.25
viscous = 0.1
F32, BF16 = jnp.float32, jnp.bfloat16
VMEM = pl.BlockSpec(memory_space=pltpu.VMEM)
HBM = pl.BlockSpec(memory_space=pltpu.MemorySpace.HBM)
LIMIT = 48 << 20
UNROLL = 4


def frequencies():
    return [0.4 * (k + 1) for k in range(NFREQ)]


def forcing_time(moment):
    return sum(math.cos(w * moment) for w in frequencies())


def call(body, outs, cost, **kw):
    shapes = [
        pltpu.MemorySpace.HBM(s, d) if spec is HBM else jax.ShapeDtypeStruct(s, d)
        for (s, d), spec in zip(outs, kw["out_specs"], strict=True)
    ]
    return pl.pallas_call(
        body,
        out_shape=shapes,
        compiler_params=pltpu.CompilerParams(vmem_limit_bytes=LIMIT),
        cost_estimate=pl.CostEstimate(flops=cost, bytes_accessed=cost, transcendentals=0),
        **kw,
    )


def parities():
    return lax.rem(lax.axis_index("ax"), 2), lax.rem(lax.axis_index("az"), 2)


def pack_rows(outer, inner, odd, first, second):
    for half, ref in enumerate((outer, inner)):
        low = ref[pl.ds(0, 80, stride=8), :]
        high = ref[pl.ds(7, 80, stride=8), :]
        where = pl.ds(half * 80, 80)
        first[where, :] = jnp.where(odd == 0, high, low)
        second[where, :] = jnp.where(odd == 0, low, high)


def run_copies(pairs, sem):
    copies = [pltpu.make_async_copy(a, b, sem.at[i]) for i, (a, b) in enumerate(pairs)]
    for copy in copies:
        copy.start()
    return copies


def halves(array, odd_x, outer, inner, pieces):
    size = NFORCE // pieces
    pairs = []
    for at, ref in ((odd_x, outer), (1 - odd_x, inner)):
        for i in range(pieces):
            part = pl.ds(i * size, size)
            pairs.append((array.at[part, :, at], ref.reshape(NFORCE, NVAR, 8, 128).at[part]))
    return pairs


def split_state(state, outer, inner, first, second, sem):
    odd_x, odd_z = parities()
    for copy in run_copies(halves(state, odd_x, outer, inner, 4), sem):
        copy.wait()
    pack_rows(outer, inner, odd_z, first, second)


def split_fixed(forcing, axial, swirl, coupling, f_out, f_in, c_out, c_in, s_out, s_in, c_all, a_all, w_all, sem):
    odd_x, _ = parities()
    sign = jnp.where(odd_x == 0, 1.0, -1.0)
    pairs = [(coupling, c_all), (axial, a_all), (swirl, w_all)]
    copies = run_copies(pairs + halves(forcing, odd_x, f_out, f_in, 4), sem)
    for copy in copies[:3]:
        copy.wait()
    for layer, c, s, toward in ((odd_x, c_out, s_out, -sign), (1 - odd_x, c_in, s_in, sign)):
        for v in range(NVAR):
            for w in range(NVAR):
                shift = 6.0 * viscous if v == w else 0.0
                c[pl.ds((v * NVAR + w) * 8, 8), :] = c_all[v, w, layer] - shift
        s[0:8, :] = a_all[layer] * (0.5 * toward)
        s[8:16, :] = w_all[layer] * 0.5
    for copy in copies[3:]:
        copy.wait()


def layer_body(inner, stage, gval, refs):
    (own, other, recv, z1, z2, forcing, coupling, speed), rest = refs[:8], refs[8:]
    odd_x, odd_z = parities()
    sign = jnp.where(odd_x == 0, 0.5, -0.5)
    if not inner:
        sign = -sign
    sub = lax.broadcasted_iota(jnp.int32, (8, 128), 0)
    lane = lax.broadcasted_iota(jnp.int32, (8, 128), 1)
    row0, row7 = sub == 0, sub == 7
    from_low = jnp.where(lane == 0, 0.0, viscous)
    from_high = jnp.where(lane == 127, 0.0, viscous)
    pick = (sub < 4) == (odd_z == 1)
    base = 80 if inner else 0
    adv, swr = speed[0:8, :], speed[8:16, :]
    c_other, c_recv = viscous + adv, viscous - adv
    c_minus, c_plus = viscous + swr, viscous - swr
    edge_of_domain = None
    if not inner:
        position = lax.axis_index("ax")
        inside = jnp.where((position > 0) & (position < 31), 1.0, 0.0)
        c_recv = c_recv * inside
        edge_of_domain = sign * inside
    c_dx = sign if inner else edge_of_domain
    if stage == 1:
        start, (out,) = own, rest[:1]
    elif stage in (2, 3):
        start, (out,) = rest[0], rest[1:2]
    else:
        start, y2, y3, out = rest[:4]
    group = 2

    def one(block, carry):
        at = [pl.multiple_of((block * group + g) * 40, 8) for g in range(group)]
        y = [[own[pl.ds(at[g] + v * 8, 8), :] for v in range(NVAR)] for g in range(group)]
        press = [{} for _ in range(group)]
        rate = [{} for _ in range(group)]
        for v in (4, 1, 2, 0, 3):
            for g in range(group):
                rows = pl.ds(at[g] + v * 8, 8)
                a, b = other[rows, :], recv[rows, :]
                n = base + (block * group + g) * NVAR + v
                edge = jnp.where(
                    pick,
                    jnp.broadcast_to(z1[pl.ds(n, 1), :], (8, 128)),
                    jnp.broadcast_to(z2[pl.ds(n, 1), :], (8, 128)),
                )
                me = y[g][v]
                tm = jnp.where(row0, edge, pltpu.roll(me, 1, 0))
                tp = jnp.where(row7, edge, pltpu.roll(me, 7, 0))
                if v in (1, 4):
                    press[g]["x", v] = b * c_dx - a * sign
                if v in (2, 4):
                    press[g]["t", v] = 0.5 * (tp - tm)
                rate[g][v] = (
                    (c_other * a + c_recv * b)
                    + (c_minus * tm + c_plus * tp)
                    + (from_low * pltpu.roll(me, 1, 1) + from_high * pltpu.roll(me, 127, 1))
                    + gval * forcing[rows, :]
                )
            for w in range(NVAR):
                c = coupling[(v * NVAR + w) * 8 : (v * NVAR + w) * 8 + 8, :]
                for g in range(group):
                    rate[g][v] = rate[g][v] + c * y[g][w]
        for g in range(group):
            rate[g][1] = rate[g][1] - press[g]["x", 4]
            rate[g][2] = rate[g][2] - press[g]["t", 4]
            rate[g][4] = rate[g][4] - (press[g]["x", 1] + press[g]["t", 2])
            for v in range(NVAR):
                rows = pl.ds(at[g] + v * 8, 8)
                q = y[g][v] if stage == 1 else start[rows, :]
                if stage < 4:
                    weight = step_size if stage == 3 else 0.5 * step_size
                    out[rows, :] = q + weight * rate[g][v]
                else:
                    mean = (y2[rows, :] - q) + (2.0 * y3[rows, :] + y[g][v])
                    out[rows, :] = mean * (1.0 / 3.0) + (step_size / 6.0) * rate[g][v]
        return carry

    lax.fori_loop(0, NFORCE // group, one, 0, unroll=UNROLL)


def outer_layer(stage, gval, *args):
    def body(*refs):
        layer_body(False, stage, gval, refs)

    return call(body, [((ROWS, 128), F32)], 1 << 20, in_specs=[VMEM] * len(args), out_specs=[VMEM])(*args)[0]


def last_layer(stage, gval, *args):
    def body(*refs):
        layer_body(True, stage, gval, refs)

    return call(body, [((ROWS, 128), F32)], 1 << 20, in_specs=[VMEM] * len(args), out_specs=[VMEM])(*args)[0]


def inner_layer(stage, gval, new_outer, *args):
    def body(done, *refs):
        layer_body(True, stage, gval, refs)
        _, odd_z = parities()
        pack_rows(done, refs[-3], odd_z, refs[-2], refs[-1])

    return call(
        body,
        [((ROWS, 128), F32), ((160, 128), F32), ((160, 128), F32)],
        1 << 20,
        in_specs=[VMEM] * (len(args) + 1),
        out_specs=[VMEM] * 3,
    )(new_outer, *args)


def swaps():
    core = [(i, i ^ 1) for i in range(32)]
    pairs = [(i, i + 1) for i in range(1, 31, 2)]
    pairs += [(b, a) for a, b in pairs]
    chip = [(a * 8 + z, b * 8 + z) for a, b in pairs for z in range(8)]
    chip += [(e * 8 + z, e * 8 + (z ^ 1)) for e in (0, 31) for z in range(8)]
    z1 = [(i, i ^ 1) for i in range(8)]
    z2 = [(i, (i + 1) % 8) for i in range(1, 8, 2)]
    z2 += [(b, a) for a, b in z2]
    return core, chip, z1, z2


def three_parts(x):
    high = x.astype(BF16)
    rest = x - high.astype(F32)
    mid = rest.astype(BF16)
    low = (rest - mid.astype(F32)).astype(BF16)
    return high, mid, low


def split_rows(ref, first, stride, parts, n, lanes, places):
    split = three_parts(ref[pl.ds(first, NFORCE, stride=stride), :])
    for place in places:
        parts[pl.ds(place * 32 + n * 16, 16), lanes] = split[(0, 1, 2, 0, 1, 0)[place]]


def gram_body(first_out, first_in, last_out, last_in, middle, final, packed, parts, sem):
    odd_x, _ = parities()
    cube = lambda ref: ref.reshape(NFORCE, NVAR, 8, 128)
    copies = [
        pltpu.make_async_copy(cube(ref), to.at[:, :, at], sem.at[i])
        for i, (ref, to, at) in enumerate(
            (
                (first_out, middle, odd_x),
                (first_in, middle, 1 - odd_x),
                (last_out, final, odd_x),
                (last_in, final, 1 - odd_x),
            )
        )
    ]
    for copy in copies:
        copy.start()
    layers = ((first_out, last_out), (first_in, last_in))
    total = jnp.zeros((96, 96), F32)
    for v in range(NVAR):
        for half, pair in enumerate(layers):
            for t in range(8):
                lanes = pl.ds(half * 1024 + t * 128, 128)
                for n, ref in enumerate(pair):
                    split_rows(ref, v * 8 + t, 40, parts.at[v], n, lanes, (0, 1, 2))
        block = parts[v]
        total = total + lax.dot_general(
            block, block, (((1,), (1,)), ((), ())), preferred_element_type=F32
        )
    small = total[0:32] + total[32:64] + total[64:96]
    small = small[:, 0:32] + small[:, 32:64] + small[:, 64:96]
    flat = jnp.concatenate([small[8 * a : 8 * a + 8] for a in range(4)], axis=1)
    for i in range(32):
        packed[i] = flat
    for copy in copies:
        copy.wait()


def gram_parts(first_out, first_in, last_out, last_in):
    state = ((NFORCE, NVAR, 2, 8, 128), F32)
    return call(
        gram_body,
        [state, state, ((32, 8, 128), F32)],
        1 << 22,
        in_specs=[VMEM] * 4,
        out_specs=[HBM] * 2 + [VMEM],
        scratch_shapes=[pltpu.VMEM((NVAR, 96, 2048), BF16), pltpu.SemaphoreType.DMA((4,))],
    )(first_out, first_in, last_out, last_in)


def lane_tables():
    rows = []
    for k, w in enumerate(frequencies()):
        for j in range(NFORCE):
            for c in range(2):
                f = math.cos if c == 0 else (lambda a: -math.sin(a))
                rows.append(
                    (
                        math.cos(w * step_size),
                        float(j),
                        f(w * step_size) * step_size,
                        f(w * 2 * step_size) * step_size,
                    )
                )
    table = np.zeros((8, 256), np.float32)
    table[:4] = np.array(rows).T
    return table


def factor(gathered, table, weights, upper, work):
    gram = gathered[0]
    for i in range(1, 8):
        gram = gram + gathered[i]
    cells = 64.0 * 64.0 * 128.0
    gram = gram * (step_size * step_size / cells)
    both = gram + pltpu.roll(gram, 48, 1)
    cross = pltpu.roll(gram, 112, 1) + pltpu.roll(gram, 64, 1)
    cosine = table[0:1, :]
    wanted = table[1:2, :]
    rows, inv = [], []
    sub = lax.broadcasted_iota(jnp.int32, (16, 256), 0)
    for i in range(NFORCE):
        column = lambda m: jnp.concatenate(
            [jnp.broadcast_to(m[:, a * 32 + i : a * 32 + i + 1], (8, 256)) for a in range(2)], axis=0
        )
        rows.append(column(both) + cosine * column(cross))
        inv.append(jnp.where(sub == i, 1.0, 0.0))
    low = jnp.zeros((16, 256), F32)
    up = jnp.zeros((16, 256), F32)
    for p in range(NFORCE):
        pivot = rows[p][p : p + 1, :]
        scaled = rows[p] * (1.0 / pivot)
        root = lax.rsqrt(pivot)
        root = root * (1.5 - 0.5 * pivot * root * root)
        mine = wanted == float(p)
        low = jnp.where(mine, inv[p] * root, low)
        up = jnp.where(mine & (sub >= p), rows[p] * root, up)
        for i in range(p + 1, NFORCE):
            m = scaled[i : i + 1, :]
            rows[i] = rows[i] - m * rows[p]
            inv[i] = inv[i] - m * inv[p]
    side = jnp.concatenate([low * table[2:3, :], low * table[3:4, :]], axis=0)
    high, mid, tail = (x.astype(F32) for x in three_parts(side))
    stack = jnp.concatenate([high, high, high, mid, mid, tail, up, jnp.zeros((48, 256), F32)], axis=0)
    turned = stack.T
    weights[...] = turned[:, 0:192].astype(BF16)
    work[...] = turned[:, 128:256]
    upper[...] = work[pl.ds(0, 128, stride=2), :][:, 64:80].reshape(NFREQ, NFORCE, NFORCE)


def basis_body(gathered, table, middle, final, basis, upper, states, weights, work, parts, blocks, sem_in, sem_out):
    arriving = [
        [
            pltpu.make_async_copy(ref.at[:, v], states.at[n, v], sem_in.at[n, v])
            for n, ref in enumerate((middle, final))
        ]
        for v in range(NVAR)
    ]
    for pair in arriving:
        for copy in pair:
            copy.start()
    factor(gathered, table, weights, upper, work)
    leaving = []
    for v in range(NVAR):
        for n, copy in enumerate(arriving[v]):
            copy.wait()
            rows = states.at[n, v].reshape(256, 128)
            for x in range(2):
                for t in range(8):
                    lanes = pl.ds(x * 1024 + t * 128, 128)
                    split_rows(rows, x * 8 + t, 16, parts, n, lanes, range(6))
        flat = blocks.at[v].reshape(256 * 24, 128)
        for x in range(2):
            for t in range(0, 8, 2):
                lanes = pl.ds(x * 1024 + t * 128, 256)
                block = jnp.dot(weights[...], parts[:, lanes], preferred_element_type=F32)
                for u in range(2):
                    flat[pl.ds(x * 8 + t + u, 256, stride=24), :] = block[:, u * 128 : u * 128 + 128]
        for part in range(2):
            k = pl.ds(part * 4, 4)
            copy = pltpu.make_async_copy(
                blocks.at[v, k, :, :, pl.ds(0, 2)], basis.at[k, :, :, v], sem_out.at[v, part]
            )
            copy.start()
            leaving.append(copy)
    for copy in leaving:
        copy.wait()


def basis_of(gathered, middle, final):
    return call(
        basis_body,
        [
            ((NFREQ, NFORCE, 2, NVAR, 2, 8, 128), F32),
            ((NFREQ, NFORCE, NFORCE), F32),
        ],
        1 << 24,
        in_specs=[VMEM, VMEM, HBM, HBM],
        out_specs=[HBM, VMEM],
        scratch_shapes=[
            pltpu.VMEM((2, NVAR, NFORCE, 2, 8, 128), F32),
            pltpu.VMEM((256, 192), BF16),
            pltpu.VMEM((256, 128), F32),
            pltpu.VMEM((192, 2048), BF16),
            pltpu.VMEM((NVAR, NFREQ, NFORCE, 2, 3, 8, 128), F32),
            pltpu.SemaphoreType.DMA((2, NVAR)),
            pltpu.SemaphoreType.DMA((NVAR, 2)),
        ],
    )(gathered, jnp.asarray(lane_tables()), *in_hbm(middle, final))


def in_hbm(*arrays):
    return [pltpu.with_memory_space_constraint(a, pltpu.MemorySpace.HBM) for a in arrays]


def on_device(initial_state, forcing, axial_speed, swirl_speed, coupling):
    core, chip, z1, z2 = swaps()
    layer, rows = ((ROWS, 128), F32), ((160, 128), F32)
    outer, inner, first, second = call(
        split_state,
        [layer, layer, rows, rows],
        1 << 20,
        in_specs=[HBM],
        out_specs=[VMEM] * 4,
        scratch_shapes=[pltpu.SemaphoreType.DMA((8,))],
    )(*in_hbm(initial_state))
    c, s = ((200, 128), F32), ((16, 128), F32)
    f_out, f_in, c_out, c_in, s_out, s_in = call(
        split_fixed,
        [layer, layer, c, c, s, s],
        1 << 20,
        in_specs=[HBM] * 4,
        out_specs=[VMEM] * 6,
        scratch_shapes=[
            pltpu.VMEM((NVAR, NVAR, 2, 8, 128), F32),
            pltpu.VMEM((2, 8, 128), F32),
            pltpu.VMEM((2, 8, 128), F32),
            pltpu.SemaphoreType.DMA((11,)),
        ],
    )(*in_hbm(forcing, axial_speed, swirl_speed, coupling))

    kept = []
    for step in range(STEPS):
        moment = step * step_size
        times = (moment, moment + 0.5 * step_size, moment + 0.5 * step_size, moment + step_size)
        base = (outer, inner)
        history = []
        for stage in range(1, 5):
            gval = forcing_time(times[stage - 1])
            from_chip = lax.ppermute(outer, ("ax", "az"), chip)
            from_core = lax.ppermute(inner, "ax", core)
            r1 = lax.ppermute(first, "az", z1)
            r2 = lax.ppermute(second, "az", z2)
            if stage == 1:
                more = ((), ())
            elif stage < 4:
                more = ((base[0],), (base[1],))
            else:
                more = tuple((base[i], history[0][i], history[1][i]) for i in range(2))
            new_outer = outer_layer(stage, gval, outer, inner, from_chip, r1, r2, f_out, c_out, s_out, *more[0])
            here = (inner, outer, from_core, r1, r2, f_in, c_in, s_in, *more[1])
            if step == STEPS - 1 and stage == 4:
                new_inner = last_layer(stage, gval, *here)
            else:
                new_inner, first, second = inner_layer(stage, gval, new_outer, *here)
            outer, inner = new_outer, new_inner
            history.append((outer, inner))
        kept.append((outer, inner))
    middle, final, packed = gram_parts(*kept[0], *kept[1])
    gathered = lax.all_to_all(packed, "ax", 0, 0, tiled=True)
    partial = jnp.broadcast_to(jnp.sum(gathered, axis=0)[None], (8, 8, 128))
    gathered = lax.all_to_all(partial, "az", 0, 0, tiled=True)
    basis, upper = basis_of(gathered, middle, final)
    return final, basis, upper


def solution(mesh):
    return jax.shard_map(
        on_device,
        mesh=mesh,
        in_specs=(
            P(None, None, "ax", "az", None),
            P(None, None, "ax", "az", None),
            P("ax", "az", None),
            P("ax", "az", None),
            P(None, None, "ax", "az", None),
        ),
        out_specs=(
            P(None, None, "ax", "az", None),
            P(None, None, None, None, "ax", "az", None),
            P(),
        ),
        check_vma=False,
    )
```

```python
import math

import jax
import jax.numpy as jnp
import numpy as np
from jax import lax
from jax.experimental import pallas as pl
from jax.experimental.pallas import tpu as pltpu
from jax.sharding import PartitionSpec as P

NFORCE = 16
NVAR = 5
NFREQ = 8
STEPS = 2
ROWS = NFORCE * NVAR * 8
step_size = 0.25
viscous = 0.1
F32, BF16 = jnp.float32, jnp.bfloat16
VMEM = pl.BlockSpec(memory_space=pltpu.VMEM)
HBM = pl.BlockSpec(memory_space=pltpu.MemorySpace.HBM)
LIMIT = 48 << 20
UNROLL = 8


def frequencies():
    return [0.4 * (k + 1) for k in range(NFREQ)]


def forcing_time(moment):
    return sum(math.cos(w * moment) for w in frequencies())


def call(body, outs, cost, **kw):
    shapes = [
        pltpu.MemorySpace.HBM(s, d) if spec is HBM else jax.ShapeDtypeStruct(s, d)
        for (s, d), spec in zip(outs, kw["out_specs"], strict=True)
    ]
    return pl.pallas_call(
        body,
        out_shape=shapes,
        compiler_params=pltpu.CompilerParams(vmem_limit_bytes=LIMIT),
        cost_estimate=pl.CostEstimate(flops=cost, bytes_accessed=cost, transcendentals=0),
        **kw,
    )


def parities():
    return lax.rem(lax.axis_index("ax"), 2), lax.rem(lax.axis_index("az"), 2)


def pack_rows(outer, inner, odd, first, second):
    for half, ref in enumerate((outer, inner)):
        low = ref[pl.ds(0, 80, stride=8), :]
        high = ref[pl.ds(7, 80, stride=8), :]
        where = pl.ds(half * 80, 80)
        first[where, :] = jnp.where(odd == 0, high, low)
        second[where, :] = jnp.where(odd == 0, low, high)


def run_copies(pairs, sem):
    copies = [pltpu.make_async_copy(a, b, sem.at[i]) for i, (a, b) in enumerate(pairs)]
    for copy in copies:
        copy.start()
    return copies


def halves(array, odd_x, outer, inner, pieces):
    size = NFORCE // pieces
    pairs = []
    for at, ref in ((odd_x, outer), (1 - odd_x, inner)):
        for i in range(pieces):
            part = pl.ds(i * size, size)
            pairs.append((array.at[part, :, at], ref.reshape(NFORCE, NVAR, 8, 128).at[part]))
    return pairs


def split_state(state, outer, inner, first, second, sem):
    odd_x, odd_z = parities()
    for copy in run_copies(halves(state, odd_x, outer, inner, 4), sem):
        copy.wait()
    pack_rows(outer, inner, odd_z, first, second)


def split_fixed(forcing, axial, swirl, coupling, f_out, f_in, c_out, c_in, s_out, s_in, c_all, a_all, w_all, sem):
    odd_x, _ = parities()
    sign = jnp.where(odd_x == 0, 1.0, -1.0)
    pairs = [(coupling, c_all), (axial, a_all), (swirl, w_all)]
    copies = run_copies(pairs + halves(forcing, odd_x, f_out, f_in, 4), sem)
    for copy in copies[:3]:
        copy.wait()
    for layer, c, s, toward in ((odd_x, c_out, s_out, -sign), (1 - odd_x, c_in, s_in, sign)):
        for v in range(NVAR):
            for w in range(NVAR):
                shift = 6.0 * viscous if v == w else 0.0
                c[pl.ds((v * NVAR + w) * 8, 8), :] = c_all[v, w, layer] - shift
        s[0:8, :] = a_all[layer] * (0.5 * toward)
        s[8:16, :] = w_all[layer] * 0.5
    for copy in copies[3:]:
        copy.wait()


def layer_body(inner, stage, gval, refs):
    (own, other, recv, z1, z2, forcing, coupling, speed), rest = refs[:8], refs[8:]
    odd_x, odd_z = parities()
    sign = jnp.where(odd_x == 0, 0.5, -0.5)
    if not inner:
        sign = -sign
    sub = lax.broadcasted_iota(jnp.int32, (8, 128), 0)
    lane = lax.broadcasted_iota(jnp.int32, (8, 128), 1)
    row0, row7 = sub == 0, sub == 7
    from_low = jnp.where(lane == 0, 0.0, viscous)
    from_high = jnp.where(lane == 127, 0.0, viscous)
    pick = (sub < 4) == (odd_z == 1)
    base = 80 if inner else 0
    adv, swr = speed[0:8, :], speed[8:16, :]
    c_other, c_recv = viscous + adv, viscous - adv
    c_minus, c_plus = viscous + swr, viscous - swr
    edge_of_domain = None
    if not inner:
        position = lax.axis_index("ax")
        inside = jnp.where((position > 0) & (position < 31), 1.0, 0.0)
        c_recv = c_recv * inside
        edge_of_domain = sign * inside
    c_dx = sign if inner else edge_of_domain
    if stage == 1:
        start, (out,) = own, rest[:1]
    elif stage in (2, 3):
        start, (out,) = rest[0], rest[1:2]
    else:
        start, y2, y3, out = rest[:4]
    group = 2

    def one(block, carry):
        at = [pl.multiple_of((block * group + g) * 40, 8) for g in range(group)]
        y = [[own[pl.ds(at[g] + v * 8, 8), :] for v in range(NVAR)] for g in range(group)]
        press = [{} for _ in range(group)]
        rate = [{} for _ in range(group)]
        for v in (4, 1, 2, 0, 3):
            for g in range(group):
                rows = pl.ds(at[g] + v * 8, 8)
                a, b = other[rows, :], recv[rows, :]
                n = base + (block * group + g) * NVAR + v
                edge = jnp.where(
                    pick,
                    jnp.broadcast_to(z1[pl.ds(n, 1), :], (8, 128)),
                    jnp.broadcast_to(z2[pl.ds(n, 1), :], (8, 128)),
                )
                me = y[g][v]
                tm = jnp.where(row0, edge, pltpu.roll(me, 1, 0))
                tp = jnp.where(row7, edge, pltpu.roll(me, 7, 0))
                if v in (1, 4):
                    press[g]["x", v] = b * c_dx - a * sign
                if v in (2, 4):
                    press[g]["t", v] = 0.5 * (tp - tm)
                rate[g][v] = (
                    (c_other * a + c_recv * b)
                    + (c_minus * tm + c_plus * tp)
                    + (from_low * pltpu.roll(me, 1, 1) + from_high * pltpu.roll(me, 127, 1))
                    + gval * forcing[rows, :]
                )
            for w in range(NVAR):
                c = coupling[(v * NVAR + w) * 8 : (v * NVAR + w) * 8 + 8, :]
                for g in range(group):
                    rate[g][v] = rate[g][v] + c * y[g][w]
        for g in range(group):
            rate[g][1] = rate[g][1] - press[g]["x", 4]
            rate[g][2] = rate[g][2] - press[g]["t", 4]
            rate[g][4] = rate[g][4] - (press[g]["x", 1] + press[g]["t", 2])
            for v in range(NVAR):
                rows = pl.ds(at[g] + v * 8, 8)
                q = y[g][v] if stage == 1 else start[rows, :]
                if stage < 4:
                    weight = step_size if stage == 3 else 0.5 * step_size
                    out[rows, :] = q + weight * rate[g][v]
                else:
                    mean = (y2[rows, :] - q) + (2.0 * y3[rows, :] + y[g][v])
                    out[rows, :] = mean * (1.0 / 3.0) + (step_size / 6.0) * rate[g][v]
        return carry

    lax.fori_loop(0, NFORCE // group, one, 0, unroll=UNROLL)


def outer_layer(stage, gval, *args):
    def body(*refs):
        layer_body(False, stage, gval, refs)

    return call(body, [((ROWS, 128), F32)], 1 << 20, in_specs=[VMEM] * len(args), out_specs=[VMEM])(*args)[0]


def last_layer(stage, gval, *args):
    def body(*refs):
        layer_body(True, stage, gval, refs)

    return call(body, [((ROWS, 128), F32)], 1 << 20, in_specs=[VMEM] * len(args), out_specs=[VMEM])(*args)[0]


def inner_layer(stage, gval, new_outer, *args):
    def body(done, *refs):
        layer_body(True, stage, gval, refs)
        _, odd_z = parities()
        pack_rows(done, refs[-3], odd_z, refs[-2], refs[-1])

    return call(
        body,
        [((ROWS, 128), F32), ((160, 128), F32), ((160, 128), F32)],
        1 << 20,
        in_specs=[VMEM] * (len(args) + 1),
        out_specs=[VMEM] * 3,
    )(new_outer, *args)


def swaps():
    core = [(i, i ^ 1) for i in range(32)]
    pairs = [(i, i + 1) for i in range(1, 31, 2)]
    pairs += [(b, a) for a, b in pairs]
    chip = [(a * 8 + z, b * 8 + z) for a, b in pairs for z in range(8)]
    chip += [(e * 8 + z, e * 8 + (z ^ 1)) for e in (0, 31) for z in range(8)]
    z1 = [(i, i ^ 1) for i in range(8)]
    z2 = [(i, (i + 1) % 8) for i in range(1, 8, 2)]
    z2 += [(b, a) for a, b in z2]
    return core, chip, z1, z2


def three_parts(x):
    high = x.astype(BF16)
    rest = x - high.astype(F32)
    mid = rest.astype(BF16)
    low = (rest - mid.astype(F32)).astype(BF16)
    return high, mid, low


def split_rows(ref, first, stride, parts, n, lanes, places):
    split = three_parts(ref[pl.ds(first, NFORCE, stride=stride), :])
    for place in places:
        parts[pl.ds(place * 32 + n * 16, 16), lanes] = split[(0, 1, 2, 0, 1, 0)[place]]


def early_body(outer, inner, state, parts, sem):
    odd_x, _ = parities()
    copies = run_copies([(b, a) for a, b in halves(state, odd_x, outer, inner, 1)], sem)
    for v in range(NVAR):
        for half, ref in enumerate((outer, inner)):
            for t in range(8):
                lanes = pl.ds(half * 1024 + t * 128, 128)
                split_rows(ref, v * 8 + t, 40, parts.at[v], 0, lanes, (0, 1, 2))
    for copy in copies:
        copy.wait()


def early(outer, inner):
    return call(
        early_body,
        [((NFORCE, NVAR, 2, 8, 128), F32), ((NVAR, 96, 2048), BF16)],
        1 << 20,
        in_specs=[VMEM] * 2,
        out_specs=[HBM, VMEM],
        scratch_shapes=[pltpu.SemaphoreType.DMA((2,))],
    )(outer, inner)


def gram_body(outer, inner, before, final, packed, parts, sem):
    odd_x, _ = parities()
    copies = run_copies([(b, a) for a, b in halves(final, odd_x, outer, inner, 1)], sem)
    total = jnp.zeros((96, 96), F32)
    for v in range(NVAR):
        for half, ref in enumerate((outer, inner)):
            for t in range(8):
                lanes = pl.ds(half * 1024 + t * 128, 128)
                split_rows(ref, v * 8 + t, 40, parts, 1, lanes, (0, 1, 2))
        for place in range(3):
            parts[pl.ds(place * 32, 16), :] = before[v, pl.ds(place * 32, 16), :]
        block = parts[...]
        total = total + lax.dot_general(
            block, block, (((1,), (1,)), ((), ())), preferred_element_type=F32
        )
    small = total[0:32] + total[32:64] + total[64:96]
    small = small[:, 0:32] + small[:, 32:64] + small[:, 64:96]
    flat = jnp.concatenate([small[8 * a : 8 * a + 8] for a in range(4)], axis=1)
    for i in range(32):
        packed[i] = flat
    for copy in copies:
        copy.wait()


def gram_parts(outer, inner, before):
    return call(
        gram_body,
        [((NFORCE, NVAR, 2, 8, 128), F32), ((32, 8, 128), F32)],
        1 << 22,
        in_specs=[VMEM] * 3,
        out_specs=[HBM, VMEM],
        scratch_shapes=[pltpu.VMEM((96, 2048), BF16), pltpu.SemaphoreType.DMA((2,))],
    )(outer, inner, before)


def lane_tables():
    rows = []
    for k, w in enumerate(frequencies()):
        for j in range(NFORCE):
            for c in range(2):
                f = math.cos if c == 0 else (lambda a: -math.sin(a))
                rows.append(
                    (
                        math.cos(w * step_size),
                        float(j),
                        f(w * step_size) * step_size,
                        f(w * 2 * step_size) * step_size,
                    )
                )
    table = np.zeros((8, 256), np.float32)
    table[:4] = np.array(rows).T
    return table


def factor(gathered, table, weights, upper, work):
    gram = gathered[0]
    for i in range(1, 8):
        gram = gram + gathered[i]
    cells = 64.0 * 64.0 * 128.0
    gram = gram * (step_size * step_size / cells)
    both = gram + pltpu.roll(gram, 48, 1)
    cross = pltpu.roll(gram, 112, 1) + pltpu.roll(gram, 64, 1)
    cosine = table[0:1, :]
    wanted = table[1:2, :]
    rows, inv = [], []
    sub = lax.broadcasted_iota(jnp.int32, (16, 256), 0)
    for i in range(NFORCE):
        column = lambda m: jnp.concatenate(
            [jnp.broadcast_to(m[:, a * 32 + i : a * 32 + i + 1], (8, 256)) for a in range(2)], axis=0
        )
        rows.append(column(both) + cosine * column(cross))
        inv.append(jnp.where(sub == i, 1.0, 0.0))
    low = jnp.zeros((16, 256), F32)
    up = jnp.zeros((16, 256), F32)
    for p in range(NFORCE):
        pivot = rows[p][p : p + 1, :]
        scaled = rows[p] * (1.0 / pivot)
        root = lax.rsqrt(pivot)
        root = root * (1.5 - 0.5 * pivot * root * root)
        mine = wanted == float(p)
        low = jnp.where(mine, inv[p] * root, low)
        up = jnp.where(mine & (sub >= p), rows[p] * root, up)
        for i in range(p + 1, NFORCE):
            m = scaled[i : i + 1, :]
            rows[i] = rows[i] - m * rows[p]
            inv[i] = inv[i] - m * inv[p]
    side = jnp.concatenate([low * table[2:3, :], low * table[3:4, :]], axis=0)
    high, mid, tail = (x.astype(F32) for x in three_parts(side))
    stack = jnp.concatenate([high, high, high, mid, mid, tail, up, jnp.zeros((48, 256), F32)], axis=0)
    turned = stack.T
    weights[...] = turned[:, 0:192].astype(BF16)
    work[...] = turned[:, 128:256]
    upper[...] = work[pl.ds(0, 128, stride=2), :][:, 64:80].reshape(NFREQ, NFORCE, NFORCE)


def basis_body(gathered, table, middle, final, basis, upper, triangle, states, weights, work, parts, blocks, sem_in, sem_out):
    arriving = [
        [
            pltpu.make_async_copy(ref.at[:, v], states.at[n, v], sem_in.at[n, v])
            for n, ref in enumerate((middle, final))
        ]
        for v in range(NVAR)
    ]
    for pair in arriving:
        for copy in pair:
            copy.start()
    factor(gathered, table, weights, triangle, work)
    copy = pltpu.make_async_copy(triangle, upper, sem_out.at[NVAR, 0])
    copy.start()
    leaving = [copy]
    for v in range(NVAR):
        for n, copy in enumerate(arriving[v]):
            copy.wait()
            rows = states.at[n, v].reshape(256, 128)
            for x in range(2):
                for t in range(8):
                    lanes = pl.ds(x * 1024 + t * 128, 128)
                    split_rows(rows, x * 8 + t, 16, parts, n, lanes, range(6))
        flat = blocks.at[v].reshape(256 * 24, 128)
        for x in range(2):
            for t in range(0, 8, 2):
                lanes = pl.ds(x * 1024 + t * 128, 256)
                block = jnp.dot(weights[...], parts[:, lanes], preferred_element_type=F32)
                for u in range(2):
                    flat[pl.ds(x * 8 + t + u, 256, stride=24), :] = block[:, u * 128 : u * 128 + 128]
            copy = pltpu.make_async_copy(
                blocks.at[v, :, :, :, x], basis.at[:, :, :, v, x], sem_out.at[v, x]
            )
            copy.start()
            leaving.append(copy)
    for copy in leaving:
        copy.wait()


def basis_of(gathered, middle, final):
    return call(
        basis_body,
        [
            ((NFREQ, NFORCE, 2, NVAR, 2, 8, 128), F32),
            ((NFREQ, NFORCE, NFORCE), F32),
        ],
        1 << 24,
        in_specs=[VMEM, VMEM, HBM, HBM],
        out_specs=[HBM, HBM],
        scratch_shapes=[
            pltpu.VMEM((NFREQ, NFORCE, NFORCE), F32),
            pltpu.VMEM((2, NVAR, NFORCE, 2, 8, 128), F32),
            pltpu.VMEM((256, 192), BF16),
            pltpu.VMEM((256, 128), F32),
            pltpu.VMEM((192, 2048), BF16),
            pltpu.VMEM((NVAR, NFREQ, NFORCE, 2, 3, 8, 128), F32),
            pltpu.SemaphoreType.DMA((2, NVAR)),
            pltpu.SemaphoreType.DMA((NVAR + 1, 2)),
        ],
    )(gathered, jnp.asarray(lane_tables()), *in_hbm(middle, final))


def in_hbm(*arrays):
    return [pltpu.with_memory_space_constraint(a, pltpu.MemorySpace.HBM) for a in arrays]


def on_device(initial_state, forcing, axial_speed, swirl_speed, coupling):
    core, chip, z1, z2 = swaps()
    layer, rows = ((ROWS, 128), F32), ((160, 128), F32)
    outer, inner, first, second = call(
        split_state,
        [layer, layer, rows, rows],
        1 << 20,
        in_specs=[HBM],
        out_specs=[VMEM] * 4,
        scratch_shapes=[pltpu.SemaphoreType.DMA((8,))],
    )(*in_hbm(initial_state))
    c, s = ((200, 128), F32), ((16, 128), F32)
    f_out, f_in, c_out, c_in, s_out, s_in = call(
        split_fixed,
        [layer, layer, c, c, s, s],
        1 << 20,
        in_specs=[HBM] * 4,
        out_specs=[VMEM] * 6,
        scratch_shapes=[
            pltpu.VMEM((NVAR, NVAR, 2, 8, 128), F32),
            pltpu.VMEM((2, 8, 128), F32),
            pltpu.VMEM((2, 8, 128), F32),
            pltpu.SemaphoreType.DMA((11,)),
        ],
    )(*in_hbm(forcing, axial_speed, swirl_speed, coupling))

    kept = []
    for step in range(STEPS):
        moment = step * step_size
        times = (moment, moment + 0.5 * step_size, moment + 0.5 * step_size, moment + step_size)
        base = (outer, inner)
        history = []
        for stage in range(1, 5):
            gval = forcing_time(times[stage - 1])
            from_chip = lax.ppermute(outer, ("ax", "az"), chip)
            from_core = lax.ppermute(inner, "ax", core)
            r1 = lax.ppermute(first, "az", z1)
            r2 = lax.ppermute(second, "az", z2)
            if stage == 1:
                more = ((), ())
            elif stage < 4:
                more = ((base[0],), (base[1],))
            else:
                more = tuple((base[i], history[0][i], history[1][i]) for i in range(2))
            new_outer = outer_layer(stage, gval, outer, inner, from_chip, r1, r2, f_out, c_out, s_out, *more[0])
            here = (inner, outer, from_core, r1, r2, f_in, c_in, s_in, *more[1])
            if step == STEPS - 1 and stage == 4:
                new_inner = last_layer(stage, gval, *here)
            else:
                new_inner, first, second = inner_layer(stage, gval, new_outer, *here)
            outer, inner = new_outer, new_inner
            history.append((outer, inner))
        kept.append((outer, inner))
    middle, before = early(*kept[0])
    final, packed = gram_parts(*kept[1], before)
    gathered = lax.all_to_all(packed, "ax", 0, 0, tiled=True)
    partial = jnp.broadcast_to(jnp.sum(gathered, axis=0)[None], (8, 8, 128))
    gathered = lax.all_to_all(partial, "az", 0, 0, tiled=True)
    basis, upper = basis_of(gathered, middle, final)
    return final, basis, upper


def solution(mesh):
    return jax.shard_map(
        on_device,
        mesh=mesh,
        in_specs=(
            P(None, None, "ax", "az", None),
            P(None, None, "ax", "az", None),
            P("ax", "az", None),
            P("ax", "az", None),
            P(None, None, "ax", "az", None),
        ),
        out_specs=(
            P(None, None, "ax", "az", None),
            P(None, None, None, None, "ax", "az", None),
            P(),
        ),
        check_vma=False,
    )
```

```python
import math

import jax
import jax.numpy as jnp
import numpy as np
from jax import lax
from jax.experimental import pallas as pl
from jax.experimental.pallas import tpu as pltpu
from jax.sharding import PartitionSpec as P

NFORCE = 16
NVAR = 5
NFREQ = 8
STEPS = 2
ROWS = NFORCE * NVAR * 8
step_size = 0.25
viscous = 0.1
F32, BF16 = jnp.float32, jnp.bfloat16
VMEM = pl.BlockSpec(memory_space=pltpu.VMEM)
HBM = pl.BlockSpec(memory_space=pltpu.MemorySpace.HBM)
LIMIT = 48 << 20
UNROLL = 8


def frequencies():
    return [0.4 * (k + 1) for k in range(NFREQ)]


def forcing_time(moment):
    return sum(math.cos(w * moment) for w in frequencies())


def call(body, outs, cost, **kw):
    shapes = [
        pltpu.MemorySpace.HBM(s, d) if spec is HBM else jax.ShapeDtypeStruct(s, d)
        for (s, d), spec in zip(outs, kw["out_specs"], strict=True)
    ]
    return pl.pallas_call(
        body,
        out_shape=shapes,
        compiler_params=pltpu.CompilerParams(vmem_limit_bytes=LIMIT),
        cost_estimate=pl.CostEstimate(flops=cost, bytes_accessed=cost, transcendentals=0),
        **kw,
    )


def parities():
    return lax.rem(lax.axis_index("ax"), 2), lax.rem(lax.axis_index("az"), 2)


def pack_rows(outer, inner, odd, first, second):
    for half, ref in enumerate((outer, inner)):
        low = ref[pl.ds(0, 80, stride=8), :]
        high = ref[pl.ds(7, 80, stride=8), :]
        where = pl.ds(half * 80, 80)
        first[where, :] = jnp.where(odd == 0, high, low)
        second[where, :] = jnp.where(odd == 0, low, high)


def run_copies(pairs, sem):
    copies = [pltpu.make_async_copy(a, b, sem.at[i]) for i, (a, b) in enumerate(pairs)]
    for copy in copies:
        copy.start()
    return copies


def halves(array, odd_x, outer, inner, pieces):
    size = NFORCE // pieces
    pairs = []
    for at, ref in ((odd_x, outer), (1 - odd_x, inner)):
        for i in range(pieces):
            part = pl.ds(i * size, size)
            pairs.append((array.at[part, :, at], ref.reshape(NFORCE, NVAR, 8, 128).at[part]))
    return pairs


def split_state(state, outer, inner, first, second, sem):
    odd_x, odd_z = parities()
    for copy in run_copies(halves(state, odd_x, outer, inner, 4), sem):
        copy.wait()
    pack_rows(outer, inner, odd_z, first, second)


def split_fixed(forcing, axial, swirl, coupling, f_out, f_in, c_out, c_in, s_out, s_in, c_all, a_all, w_all, sem):
    odd_x, _ = parities()
    sign = jnp.where(odd_x == 0, 1.0, -1.0)
    pairs = [(coupling, c_all), (axial, a_all), (swirl, w_all)]
    copies = run_copies(pairs + halves(forcing, odd_x, f_out, f_in, 4), sem)
    for copy in copies[:3]:
        copy.wait()
    for layer, c, s, toward in ((odd_x, c_out, s_out, -sign), (1 - odd_x, c_in, s_in, sign)):
        for v in range(NVAR):
            for w in range(NVAR):
                shift = 6.0 * viscous if v == w else 0.0
                c[pl.ds((v * NVAR + w) * 8, 8), :] = c_all[v, w, layer] - shift
        s[0:8, :] = a_all[layer] * (0.5 * toward)
        s[8:16, :] = w_all[layer] * 0.5
    for copy in copies[3:]:
        copy.wait()


def layer_body(inner, stage, gval, refs):
    (own, other, recv, z1, z2, forcing, coupling, speed), rest = refs[:8], refs[8:]
    odd_x, odd_z = parities()
    sign = jnp.where(odd_x == 0, 0.5, -0.5)
    if not inner:
        sign = -sign
    sub = lax.broadcasted_iota(jnp.int32, (8, 128), 0)
    lane = lax.broadcasted_iota(jnp.int32, (8, 128), 1)
    row0, row7 = sub == 0, sub == 7
    from_low = jnp.where(lane == 0, 0.0, viscous)
    from_high = jnp.where(lane == 127, 0.0, viscous)
    pick = (sub < 4) == (odd_z == 1)
    base = 80 if inner else 0
    adv, swr = speed[0:8, :], speed[8:16, :]
    c_other, c_recv = viscous + adv, viscous - adv
    c_minus, c_plus = viscous + swr, viscous - swr
    edge_of_domain = None
    if not inner:
        position = lax.axis_index("ax")
        inside = jnp.where((position > 0) & (position < 31), 1.0, 0.0)
        c_recv = c_recv * inside
        edge_of_domain = sign * inside
    c_dx = sign if inner else edge_of_domain
    if stage == 1:
        start, (out,) = own, rest[:1]
    elif stage in (2, 3):
        start, (out,) = rest[0], rest[1:2]
    else:
        start, y2, y3, out = rest[:4]
    group = 2

    def one(block, carry):
        at = [pl.multiple_of((block * group + g) * 40, 8) for g in range(group)]
        y = [[own[pl.ds(at[g] + v * 8, 8), :] for v in range(NVAR)] for g in range(group)]
        press = [{} for _ in range(group)]
        rate = [{} for _ in range(group)]
        for v in (4, 1, 2, 0, 3):
            for g in range(group):
                rows = pl.ds(at[g] + v * 8, 8)
                a, b = other[rows, :], recv[rows, :]
                n = base + (block * group + g) * NVAR + v
                edge = jnp.where(
                    pick,
                    jnp.broadcast_to(z1[pl.ds(n, 1), :], (8, 128)),
                    jnp.broadcast_to(z2[pl.ds(n, 1), :], (8, 128)),
                )
                me = y[g][v]
                tm = jnp.where(row0, edge, pltpu.roll(me, 1, 0))
                tp = jnp.where(row7, edge, pltpu.roll(me, 7, 0))
                if v in (1, 4):
                    press[g]["x", v] = b * c_dx - a * sign
                if v in (2, 4):
                    press[g]["t", v] = 0.5 * (tp - tm)
                rate[g][v] = (
                    (c_other * a + c_recv * b)
                    + (c_minus * tm + c_plus * tp)
                    + (from_low * pltpu.roll(me, 1, 1) + from_high * pltpu.roll(me, 127, 1))
                    + gval * forcing[rows, :]
                )
            for w in range(NVAR):
                c = coupling[(v * NVAR + w) * 8 : (v * NVAR + w) * 8 + 8, :]
                for g in range(group):
                    rate[g][v] = rate[g][v] + c * y[g][w]
        for g in range(group):
            rate[g][1] = rate[g][1] - press[g]["x", 4]
            rate[g][2] = rate[g][2] - press[g]["t", 4]
            rate[g][4] = rate[g][4] - (press[g]["x", 1] + press[g]["t", 2])
            for v in range(NVAR):
                rows = pl.ds(at[g] + v * 8, 8)
                q = y[g][v] if stage == 1 else start[rows, :]
                if stage < 4:
                    weight = step_size if stage == 3 else 0.5 * step_size
                    out[rows, :] = q + weight * rate[g][v]
                else:
                    mean = (y2[rows, :] - q) + (2.0 * y3[rows, :] + y[g][v])
                    out[rows, :] = mean * (1.0 / 3.0) + (step_size / 6.0) * rate[g][v]
        return carry

    lax.fori_loop(0, NFORCE // group, one, 0, unroll=UNROLL)


def outer_layer(stage, gval, *args):
    def body(*refs):
        layer_body(False, stage, gval, refs)

    return call(body, [((ROWS, 128), F32)], 1 << 20, in_specs=[VMEM] * len(args), out_specs=[VMEM])(*args)[0]


def last_layer(stage, gval, *args):
    def body(*refs):
        layer_body(True, stage, gval, refs)

    return call(body, [((ROWS, 128), F32)], 1 << 20, in_specs=[VMEM] * len(args), out_specs=[VMEM])(*args)[0]


def inner_layer(stage, gval, new_outer, *args):
    def body(done, *refs):
        layer_body(True, stage, gval, refs)
        _, odd_z = parities()
        pack_rows(done, refs[-3], odd_z, refs[-2], refs[-1])

    return call(
        body,
        [((ROWS, 128), F32), ((160, 128), F32), ((160, 128), F32)],
        1 << 20,
        in_specs=[VMEM] * (len(args) + 1),
        out_specs=[VMEM] * 3,
    )(new_outer, *args)


def swaps():
    core = [(i, i ^ 1) for i in range(32)]
    pairs = [(i, i + 1) for i in range(1, 31, 2)]
    pairs += [(b, a) for a, b in pairs]
    chip = [(a * 8 + z, b * 8 + z) for a, b in pairs for z in range(8)]
    chip += [(e * 8 + z, e * 8 + (z ^ 1)) for e in (0, 31) for z in range(8)]
    z1 = [(i, i ^ 1) for i in range(8)]
    z2 = [(i, (i + 1) % 8) for i in range(1, 8, 2)]
    z2 += [(b, a) for a, b in z2]
    return core, chip, z1, z2


def three_parts(x):
    high = x.astype(BF16)
    rest = x - high.astype(F32)
    mid = rest.astype(BF16)
    low = (rest - mid.astype(F32)).astype(BF16)
    return high, mid, low


def split_rows(ref, first, stride, parts, n, lanes, places):
    split = three_parts(ref[pl.ds(first, NFORCE, stride=stride), :])
    for place in places:
        parts[pl.ds(place * 32 + n * 16, 16), lanes] = split[(0, 1, 2, 0, 1, 0)[place]]


def early_body(outer, inner, state, parts, sem):
    odd_x, _ = parities()
    copies = run_copies([(b, a) for a, b in halves(state, odd_x, outer, inner, 1)], sem)
    for v in range(NVAR):
        for half, ref in enumerate((outer, inner)):
            for t in range(8):
                lanes = pl.ds(half * 1024 + t * 128, 128)
                split_rows(ref, v * 8 + t, 40, parts.at[v], 0, lanes, (0, 1, 2))
    for copy in copies:
        copy.wait()


def early(outer, inner):
    return call(
        early_body,
        [((NFORCE, NVAR, 2, 8, 128), F32), ((NVAR, 96, 2048), BF16)],
        1 << 20,
        in_specs=[VMEM] * 2,
        out_specs=[HBM, VMEM],
        scratch_shapes=[pltpu.SemaphoreType.DMA((2,))],
    )(outer, inner)


def gram_body(outer, inner, before, final, packed, parts, sem):
    odd_x, _ = parities()
    copies = run_copies([(b, a) for a, b in halves(final, odd_x, outer, inner, 1)], sem)
    total = jnp.zeros((96, 96), F32)
    for v in range(NVAR):
        for half, ref in enumerate((outer, inner)):
            for t in range(8):
                lanes = pl.ds(half * 1024 + t * 128, 128)
                split_rows(ref, v * 8 + t, 40, parts, 1, lanes, (0, 1, 2))
        for place in range(3):
            parts[pl.ds(place * 32, 16), :] = before[v, pl.ds(place * 32, 16), :]
        block = parts[...]
        total = total + lax.dot_general(
            block, block, (((1,), (1,)), ((), ())), preferred_element_type=F32
        )
    small = total[0:32] + total[32:64] + total[64:96]
    small = small[:, 0:32] + small[:, 32:64] + small[:, 64:96]
    flat = jnp.concatenate([small[8 * a : 8 * a + 8] for a in range(4)], axis=1)
    for i in range(32):
        packed[i] = flat
    for copy in copies:
        copy.wait()


def gram_parts(outer, inner, before):
    return call(
        gram_body,
        [((NFORCE, NVAR, 2, 8, 128), F32), ((32, 8, 128), F32)],
        1 << 22,
        in_specs=[VMEM] * 3,
        out_specs=[HBM, VMEM],
        scratch_shapes=[pltpu.VMEM((96, 2048), BF16), pltpu.SemaphoreType.DMA((2,))],
    )(outer, inner, before)


def lane_tables():
    rows = []
    for k, w in enumerate(frequencies()):
        for j in range(NFORCE):
            for c in range(2):
                f = math.cos if c == 0 else (lambda a: -math.sin(a))
                rows.append(
                    (
                        math.cos(w * step_size),
                        float(j),
                        f(w * step_size) * step_size,
                        f(w * 2 * step_size) * step_size,
                    )
                )
    table = np.zeros((8, 256), np.float32)
    table[:4] = np.array(rows).T
    return table


def factor(gathered, table, weights, upper, work):
    gram = gathered[0]
    for i in range(1, 8):
        gram = gram + gathered[i]
    cells = 64.0 * 64.0 * 128.0
    gram = gram * (step_size * step_size / cells)
    both = gram + pltpu.roll(gram, 48, 1)
    cross = pltpu.roll(gram, 112, 1) + pltpu.roll(gram, 64, 1)
    cosine = table[0:1, :]
    wanted = table[1:2, :]
    rows, inv = [], []
    sub = lax.broadcasted_iota(jnp.int32, (16, 256), 0)
    for i in range(NFORCE):
        column = lambda m: jnp.concatenate(
            [jnp.broadcast_to(m[:, a * 32 + i : a * 32 + i + 1], (8, 256)) for a in range(2)], axis=0
        )
        rows.append(column(both) + cosine * column(cross))
        inv.append(jnp.where(sub == i, 1.0, 0.0))
    low = jnp.zeros((16, 256), F32)
    up = jnp.zeros((16, 256), F32)
    for p in range(NFORCE):
        pivot = rows[p][p : p + 1, :]
        scaled = rows[p] * (1.0 / pivot)
        root = lax.rsqrt(pivot)
        root = root * (1.5 - 0.5 * pivot * root * root)
        mine = wanted == float(p)
        low = jnp.where(mine, inv[p] * root, low)
        up = jnp.where(mine & (sub >= p), rows[p] * root, up)
        for i in range(p + 1, NFORCE):
            m = scaled[i : i + 1, :]
            rows[i] = rows[i] - m * rows[p]
            inv[i] = inv[i] - m * inv[p]
    side = jnp.concatenate([low * table[2:3, :], low * table[3:4, :]], axis=0)
    high, mid, tail = (x.astype(F32) for x in three_parts(side))
    stack = jnp.concatenate([high, high, high, mid, mid, tail, up, jnp.zeros((48, 256), F32)], axis=0)
    turned = stack.T
    weights[...] = turned[:, 0:192].astype(BF16)
    work[...] = turned[:, 128:256]
    upper[...] = work[pl.ds(0, 128, stride=2), :][:, 64:80].reshape(NFREQ, NFORCE, NFORCE)


def basis_body(gathered, table, middle, final, basis, upper, triangle, states, weights, work, parts, blocks, sem_in, sem_out):
    arriving = [
        [
            pltpu.make_async_copy(ref.at[:, v], states.at[n, v], sem_in.at[n, v])
            for n, ref in enumerate((middle, final))
        ]
        for v in range(NVAR)
    ]
    for pair in arriving:
        for copy in pair:
            copy.start()
    factor(gathered, table, weights, triangle, work)
    copy = pltpu.make_async_copy(triangle, upper, sem_out.at[NVAR, 0])
    copy.start()
    leaving = [copy]
    for v in range(NVAR):
        for n, copy in enumerate(arriving[v]):
            copy.wait()
            rows = states.at[n, v].reshape(256, 128)
            for x in range(2):
                for t in range(8):
                    lanes = pl.ds(x * 1024 + t * 128, 128)
                    split_rows(rows, x * 8 + t, 16, parts, n, lanes, range(6))
        flat = blocks.at[v].reshape(256 * 24, 128)
        cuts = 2 if v == 0 else 1
        size = 256 // cuts
        for x in range(2):
            for cut in range(cuts):
                for t in range(0, 8, 2):
                    lanes = pl.ds(x * 1024 + t * 128, 256)
                    rows = weights[cut * size : cut * size + size, :]
                    block = jnp.dot(rows, parts[:, lanes], preferred_element_type=F32)
                    for u in range(2):
                        to = pl.ds(cut * size * 24 + x * 8 + t + u, size, stride=24)
                        flat[to, :] = block[:, u * 128 : u * 128 + 128]
                k = pl.ds(cut * (NFREQ // cuts), NFREQ // cuts)
                copy = pltpu.make_async_copy(
                    blocks.at[v, k, :, :, x], basis.at[k, :, :, v, x], sem_out.at[v, x * 2 + cut]
                )
                copy.start()
                leaving.append(copy)
    for copy in leaving:
        copy.wait()


def basis_of(gathered, middle, final):
    return call(
        basis_body,
        [
            ((NFREQ, NFORCE, 2, NVAR, 2, 8, 128), F32),
            ((NFREQ, NFORCE, NFORCE), F32),
        ],
        1 << 24,
        in_specs=[VMEM, VMEM, HBM, HBM],
        out_specs=[HBM, HBM],
        scratch_shapes=[
            pltpu.VMEM((NFREQ, NFORCE, NFORCE), F32),
            pltpu.VMEM((2, NVAR, NFORCE, 2, 8, 128), F32),
            pltpu.VMEM((256, 192), BF16),
            pltpu.VMEM((256, 128), F32),
            pltpu.VMEM((192, 2048), BF16),
            pltpu.VMEM((NVAR, NFREQ, NFORCE, 2, 3, 8, 128), F32),
            pltpu.SemaphoreType.DMA((2, NVAR)),
            pltpu.SemaphoreType.DMA((NVAR + 1, 4)),
        ],
    )(gathered, jnp.asarray(lane_tables()), *in_hbm(middle, final))


def in_hbm(*arrays):
    return [pltpu.with_memory_space_constraint(a, pltpu.MemorySpace.HBM) for a in arrays]


def on_device(initial_state, forcing, axial_speed, swirl_speed, coupling):
    core, chip, z1, z2 = swaps()
    layer, rows = ((ROWS, 128), F32), ((160, 128), F32)
    outer, inner, first, second = call(
        split_state,
        [layer, layer, rows, rows],
        1 << 20,
        in_specs=[HBM],
        out_specs=[VMEM] * 4,
        scratch_shapes=[pltpu.SemaphoreType.DMA((8,))],
    )(*in_hbm(initial_state))
    c, s = ((200, 128), F32), ((16, 128), F32)
    f_out, f_in, c_out, c_in, s_out, s_in = call(
        split_fixed,
        [layer, layer, c, c, s, s],
        1 << 20,
        in_specs=[HBM] * 4,
        out_specs=[VMEM] * 6,
        scratch_shapes=[
            pltpu.VMEM((NVAR, NVAR, 2, 8, 128), F32),
            pltpu.VMEM((2, 8, 128), F32),
            pltpu.VMEM((2, 8, 128), F32),
            pltpu.SemaphoreType.DMA((11,)),
        ],
    )(*in_hbm(forcing, axial_speed, swirl_speed, coupling))

    kept = []
    for step in range(STEPS):
        moment = step * step_size
        times = (moment, moment + 0.5 * step_size, moment + 0.5 * step_size, moment + step_size)
        base = (outer, inner)
        history = []
        for stage in range(1, 5):
            gval = forcing_time(times[stage - 1])
            from_chip = lax.ppermute(outer, ("ax", "az"), chip)
            from_core = lax.ppermute(inner, "ax", core)
            r1 = lax.ppermute(first, "az", z1)
            r2 = lax.ppermute(second, "az", z2)
            if stage == 1:
                more = ((), ())
            elif stage < 4:
                more = ((base[0],), (base[1],))
            else:
                more = tuple((base[i], history[0][i], history[1][i]) for i in range(2))
            new_outer = outer_layer(stage, gval, outer, inner, from_chip, r1, r2, f_out, c_out, s_out, *more[0])
            here = (inner, outer, from_core, r1, r2, f_in, c_in, s_in, *more[1])
            if step == STEPS - 1 and stage == 4:
                new_inner = last_layer(stage, gval, *here)
            else:
                new_inner, first, second = inner_layer(stage, gval, new_outer, *here)
            outer, inner = new_outer, new_inner
            history.append((outer, inner))
        kept.append((outer, inner))
    middle, before = early(*kept[0])
    final, packed = gram_parts(*kept[1], before)
    gathered = lax.all_to_all(packed, "ax", 0, 0, tiled=True)
    partial = jnp.broadcast_to(jnp.sum(gathered, axis=0)[None], (8, 8, 128))
    gathered = lax.all_to_all(partial, "az", 0, 0, tiled=True)
    basis, upper = basis_of(gathered, middle, final)
    return final, basis, upper


def solution(mesh):
    return jax.shard_map(
        on_device,
        mesh=mesh,
        in_specs=(
            P(None, None, "ax", "az", None),
            P(None, None, "ax", "az", None),
            P("ax", "az", None),
            P("ax", "az", None),
            P(None, None, "ax", "az", None),
        ),
        out_specs=(
            P(None, None, "ax", "az", None),
            P(None, None, None, None, "ax", "az", None),
            P(),
        ),
        check_vma=False,
    )
```
